32 devices in a mesh: grp: 8 (over z, core), tp: 4 (over y, x).
Axes of the slice: x: 2, y: 2, z: 4, core: 2. Of those that a mesh axis runs over, the one named last changes fastest.
Arguments:
- tokens: bfloat16 [8192, 1280], P('grp', 'tp'), may hold values from -40 to 40
- segment: int32 [8192], P('grp'), may hold values from 0 to 31, as said below
- ln_gain: float32 [1280], replicated, may hold values from 0.1 to 1.9
- w_qkv: bfloat16 [3, 1280, 1280], P(None, None, 'tp'), may hold values from -4.6 to 4.6
- w_out: bfloat16 [1280, 1280], P('tp'), may hold values from -0.25 to 0.25
- merge_gain: float32 [1280], replicated, may hold values from 0.1 to 1.9
- w_merge: bfloat16 [4, 1280, 1280], P(None, 'tp'), may hold values from -0.078125 to 0.078125
- owner: int32 [2048, 1], P('grp'), may hold values from 0 to 7; in each aligned block of 256 rows (0 to 255, 256 to 511, ...) at most 64 rows name the same one
Outputs:
- hidden_out: bfloat16 [8192, 1280], P('grp', 'tp')
- routed: bfloat16 [8, 8, 64, 1280], P('grp', None, None, 'tp')
The draws below stay inside these ranges and needn't reach their ends.
Inputs may be any that keep to these rules, and one draw needn't show every extreme that they name: `segment`: along each group's rows the ids never fall and come in runs of whole multiples of 4 rows, each run of 4 being one 2x2 patch block of that image; rows of one id lie in one group g or in the two groups g and g + 4, and every group shares one image with that partner group. Among the merged blocks of one group no owner is named more than 64 times; in some group one owner is named exactly 64 times.
All inputs are finite; a program needn't handle non-finite values.
Results may differ from the reference program's by a relative error of at most 0.023.
Values may be sent and summed in bfloat16 or wider, within the bound.
No kernel may reach another device: no remote copies, remote signals or barrier semaphores. Data moves between devices by JAX's collectives and lax.ppermute only.
A program may use at most 64 MiB of HBM per device.

```python
import math
import jax
import jax.numpy as jnp
import numpy as np
from jax import lax

D = 1280
H = 16
HD = 80
TOK_GRP = 1024
TOKENS = 8192
MERGED_GRP = 256
MERGED = 2048
CAP = 64
N_GRP = 8
N_TP = 4


def segment_table(key):
    pair_count = N_GRP // 2
    unit_count = TOK_GRP // 2
    margin_units = unit_count // 8

    def one_pair(pair_key):
        shuffled = jax.random.permutation(pair_key, unit_count - 1).astype(jnp.int32)
        position = jnp.arange(1, unit_count, dtype=jnp.int32)
        middle = unit_count // 2
        banned = jnp.logical_and(position >= middle - margin_units, position <= middle + margin_units)
        rank_score = shuffled + banned.astype(jnp.int32) * unit_count
        best_values, chosen_index = lax.top_k(-rank_score, 7)
        cut_units = position[chosen_index]
        cut_marks = jnp.sum((jnp.arange(unit_count, dtype=jnp.int32)[:, None] == cut_units[None, :]).astype(jnp.int32), axis=1)
        local_ids = jnp.cumsum(cut_marks).astype(jnp.int32)
        return jnp.repeat(local_ids, 4)
    pair_keys = jax.random.split(jax.random.fold_in(key, 17), pair_count)
    id_table = jax.vmap(one_pair)(pair_keys) + (jnp.arange(pair_count, dtype=jnp.int32) * 8)[:, None]
    return jnp.transpose(id_table.reshape(pair_count, 2, TOK_GRP), (1, 0, 2)).reshape(N_GRP * TOK_GRP)


def draw_segment(key, part):
    return segment_table(key).astype(jnp.int32)


def draw_tokens(key, part):
    noise_key = jax.random.fold_in(jax.random.fold_in(key, 3), 0)
    base = jnp.clip(jax.random.normal(noise_key, (TOKENS, D), jnp.float32), -4.0, 4.0)
    return base.astype(jnp.bfloat16)


def draw_w_qkv(key, part):
    noise_key = jax.random.fold_in(jax.random.fold_in(key, 5), 0)
    base = jnp.clip(jax.random.normal(noise_key, (3, D, D), jnp.float32), -4.0, 4.0) * D ** (-0.5)
    return base.astype(jnp.bfloat16)


def spiked(entries, key, source, target, parts, factor):
    def block_of(dim):
        return (jnp.arange(entries.shape[dim]) // (entries.shape[dim] // parts)).reshape((-1,) + (1,) * (entries.ndim - 1 - dim))

    first = jax.random.permutation(key, parts)[block_of(target)]
    far = (block_of(target) + parts // 2) % parts
    return jnp.where((block_of(source) == first) | (block_of(source) == far), factor * entries, entries)


def steps_of(own_key, shape, shards, low, high):
    factor_of, own = 1.0, jax.random.fold_in(own_key, 6)
    for dim, parts in shards:
        steps = jnp.exp(jax.random.uniform(jax.random.fold_in(own, dim), (parts,), jnp.float32, low / len(shards), high / len(shards)))
        factor_of = factor_of * jnp.repeat(steps, shape[dim] // parts).reshape([-1 if axis == dim else 1 for axis in range(len(shape))])
    return factor_of


def assign_block(own_key, own, number, rows, amount, top, limit, lean):
    order = jax.random.permutation(own_key, amount)
    packed, ordinary = load_shares(amount, rows * top, limit, lean, True), load_shares(amount, rows * top, limit, lean, False)
    places = jnp.arange(amount)

    def named(tallies, turn):
        used = int((tallies > 0).sum())
        fixed = max(1, used // 4)
        passed = fixed + (places - fixed + turn * (used - fixed)) % max(1, amount - fixed)
        return jnp.zeros((amount,), jnp.int32).at[order[jnp.where(places < fixed, places, passed)]].set(jnp.asarray(tallies, jnp.int32))

    tallies = jnp.where(number % 4 == 0, named(packed, number // 4), named(ordinary, number - number // 4 - 1))
    mixed = jax.random.permutation(jax.random.fold_in(own, 3), amount)
    giver, taker = mixed[0:amount // 2 * 2:2], mixed[1:amount // 2 * 2:2]
    slack = jnp.minimum(tallies[giver] - 1, limit - tallies[taker]) // 2
    slack = jnp.where((giver == order[0]) | (taker == order[0]) | (tallies[taker] == 0), 0, jnp.maximum(slack, 0))
    passed = jax.random.randint(jax.random.fold_in(own, 4), (amount // 2,), 0, 1 << 20) % (slack + 1)
    tallies = tallies.at[giver].add(-passed).at[taker].add(passed)
    members = jnp.searchsorted(jnp.cumsum(tallies), jnp.arange(rows * top), side="right").astype(jnp.int32)
    listing = members.reshape(top, rows).T
    listing = listing[jax.random.permutation(jax.random.fold_in(own, 1), rows)]
    turn = jax.random.randint(jax.random.fold_in(own, 2), (rows, 1), 0, top)
    return jnp.take_along_axis(listing, (jnp.arange(top)[None, :] + turn) % top, axis=1)


def load_shares(number_of, total, limit, lean, full):
    portions = [(1 << 20) // math.isqrt(standing ** lean) + 1 for standing in range(1, number_of + 1)]
    largest = limit if full else min(limit, max(-(-total // number_of), total * portions[0] // sum(portions)))
    least = 1 if total - largest >= number_of - 1 else 0
    holding, spare = [largest] + [least] * (number_of - 1), total - largest - least * (number_of - 1)
    while spare > 0:
        candidates = [i for i in range(1, number_of) if holding[i] < largest] or [i for i in range(1, number_of) if holding[i] < limit]
        mass, remaining = sum([portions[i] for i in candidates]), spare
        for i in candidates:
            addition = min(limit - holding[i], max(1, remaining * portions[i] // mass), spare)
            holding[i] = holding[i] + addition
            spare = spare - addition
    return np.array(holding)


def scatter_about(rng, dims, scale, most, shards=(), held_as=jnp.bfloat16):
    loudness = steps_of(rng, dims, shards, -0.22, 0.18) if shards else 1.0
    entries = jax.random.normal(rng, dims, jnp.float32) * scale * loudness
    return jnp.minimum(jnp.maximum(entries, -most), most).astype(held_as)


def heavy_noise(rng, extent, scale, limit, cuts, heavy, kind=jnp.bfloat16):
    values = scale * jax.random.normal(rng, extent, jnp.float32)
    if cuts:
        values = values * steps_of(rng, extent, cuts, -0.22, 0.18)
    return jnp.clip(spiked(values, jax.random.fold_in(rng, 3), *heavy), -limit, limit).astype(kind)


def setup_inputs(seed: int = 0) -> dict:
    seeds = jax.random.split(jax.random.key(seed), 9)
    tokens = draw_tokens(jax.random.fold_in(seeds[8], 71), 0)
    segment = draw_segment(jax.random.fold_in(seeds[8], 71), 0)
    ln_gain = jnp.clip(1.0 + 0.18 * jax.random.normal(seeds[2], (D,), jnp.float32), 0.1, 1.9)
    w_qkv = draw_w_qkv(jax.random.fold_in(seeds[8], 71), 0)
    w_out = heavy_noise(seeds[4], (D, D), D ** -0.5, 0.25, ((0, 4),), (0, 1, 4, 2.0))
    merge_gain = jnp.clip(1.0 + 0.18 * jax.random.normal(seeds[5], (D,), jnp.float32), 0.1, 1.9)
    w_merge = scatter_about(seeds[6], (4, D, D), (4 * D) ** -0.5, 0.078125, ((1, 4),))
    owner_keys = jax.random.split(jax.random.fold_in(seeds[7], 1), MERGED // MERGED_GRP)
    owner_turns = jax.random.permutation(jax.random.fold_in(seeds[7], 3), MERGED // MERGED_GRP)
    owner = jax.vmap(lambda own, number: assign_block(jax.random.fold_in(seeds[7], 2), own, number, MERGED_GRP, N_GRP, 1, CAP, 1))(owner_keys, owner_turns).reshape((MERGED, 1))
    return {"tokens": tokens, "segment": segment, "ln_gain": ln_gain, "w_qkv": w_qkv, "w_out": w_out, "merge_gain": merge_gain, "w_merge": w_merge, "owner": owner}


EPS = 1e-06

def layer_norm(rows_in, gain):
    values_f = rows_in.astype(jnp.float32)
    center = lax.optimization_barrier(jnp.mean(values_f, axis=-1, keepdims=True))
    spread = lax.optimization_barrier(jnp.mean((values_f - center) ** 2, axis=-1, keepdims=True))
    return (values_f - center) * lax.rsqrt(spread + EPS) * gain

def as_rounded(values_f):
    return lax.optimization_barrier(values_f.astype(jnp.bfloat16)).astype(jnp.float32)

def reference(tokens, segment, ln_gain, w_qkv, w_out, merge_gain, w_merge, owner):
    width_part = D // N_TP
    normed = layer_norm(tokens, ln_gain).astype(jnp.bfloat16)
    projected = jnp.stack([jnp.dot(normed, w_qkv[index], preferred_element_type=jnp.float32).astype(jnp.bfloat16) for index in range(3)])
    by_group = projected.reshape(3, N_GRP, TOK_GRP, H, HD)
    seg_groups = segment.reshape(N_GRP, TOK_GRP)
    half_count = N_GRP // 2

    def one_group(group):
        partner = (group + half_count) % N_GRP
        query_rows = by_group[0, group].astype(jnp.float32)
        key_rows = jnp.concatenate([by_group[1, group], by_group[1, partner]], axis=0).astype(jnp.float32)
        value_rows = jnp.concatenate([by_group[2, group], by_group[2, partner]], axis=0).astype(jnp.float32)
        query_seg = seg_groups[group]
        key_seg = jnp.concatenate([seg_groups[group], seg_groups[partner]], axis=0)
        score_all = jnp.einsum('qhd,khd->hqk', query_rows, key_rows) * HD ** (-0.5)
        allowed = (query_seg[:, None] == key_seg[None, :])[None]
        score_all = jnp.where(allowed, score_all, -1e+30)
        row_top = lax.optimization_barrier(jnp.max(score_all, axis=2, keepdims=True))
        raw_weights = jnp.exp(score_all - row_top)
        sums_total = lax.optimization_barrier(jnp.sum(raw_weights, axis=2))
        mixed_rows = jnp.einsum('hqk,khd->qhd', as_rounded(raw_weights), value_rows)
        return (mixed_rows / jnp.transpose(sums_total)[:, :, None]).astype(jnp.bfloat16).reshape(TOK_GRP, D)
    context = lax.map(one_group, jnp.arange(N_GRP, dtype=jnp.int32)).reshape(TOKENS, D)
    accumulated = tokens.astype(jnp.float32)
    for part_index in range(N_TP):
        low_col = part_index * width_part
        term = jnp.dot(context[:, low_col:low_col + width_part], w_out[low_col:low_col + width_part, :], preferred_element_type=jnp.float32)
        accumulated = accumulated + as_rounded(term)
    hidden_out = accumulated.astype(jnp.bfloat16)
    merge_normed = layer_norm(hidden_out, merge_gain).astype(jnp.bfloat16).reshape(MERGED, 4, D)
    merged_acc = jnp.zeros((MERGED, D), jnp.float32)
    for part_index in range(N_TP):
        low_col = part_index * width_part
        term = jnp.einsum('mjf,jfe->me', merge_normed[:, :, low_col:low_col + width_part].astype(jnp.float32), w_merge[:, low_col:low_col + width_part, :].astype(jnp.float32))
        merged_acc = merged_acc + as_rounded(term)
    merged_out = merged_acc.astype(jnp.bfloat16)
    merged_groups = merged_out.reshape(N_GRP, MERGED_GRP, D)
    owner_groups = owner.reshape(N_GRP, MERGED_GRP)

    def route(pair_in):
        group_rows, targets = pair_in
        onehot = (targets[:, None] == jnp.arange(N_GRP, dtype=jnp.int32)[None, :]).astype(jnp.float32)
        earlier = jnp.cumsum(onehot, axis=0) - onehot
        slot_index = lax.optimization_barrier(jnp.sum(earlier * onehot, axis=1)).astype(jnp.int32)
        slot_place = targets * CAP + slot_index
        dispatch = (jnp.arange(N_GRP * CAP, dtype=jnp.int32)[:, None] == slot_place[None, :]).astype(jnp.bfloat16)
        return jnp.dot(dispatch, group_rows, preferred_element_type=jnp.float32).astype(jnp.bfloat16).reshape(N_GRP, CAP, D)
    routed = lax.map(route, (merged_groups, owner_groups))
    return (hidden_out, jnp.transpose(routed, (1, 0, 2, 3)))
```

```python
import functools
import math

import jax
import jax.numpy as jnp
from jax import lax
from jax.experimental import pallas as pl
from jax.experimental.pallas import tpu as pltpu
from jax.sharding import PartitionSpec as P

HD = 80
PAD = 128
CODE_BITS = 16
FAR = 2.0**100
EPS = 1e-06
BLOCK = 256
BF = jnp.bfloat16
F32 = jnp.float32


def hop(x, axis, distance):
    return lax.ppermute(x, axis, [(i, i ^ distance) for i in range(lax.axis_size(axis))])


def params(limit):
    return pltpu.CompilerParams(vmem_limit_bytes=limit << 20)


def project_body(n_parts, n_proj, heads, scale, *refs):
    parts = refs[:n_parts]
    gain, w, qcode, kcode = refs[n_parts : n_parts + 4]
    outs = refs[n_parts + 4 : n_parts + 4 + n_proj]
    normed = refs[-1]
    values = [p[...].astype(F32) for p in parts]
    width = values[0].shape[1]
    total = width * n_parts
    center = sum(jnp.sum(v, axis=1, keepdims=True) for v in values) * (1.0 / total)
    values = [v - center for v in values]
    spread = sum(jnp.sum(v * v, axis=1, keepdims=True) for v in values) * (1.0 / total)
    inv = lax.rsqrt(spread + EPS)
    for k, v in enumerate(values):
        lo = k * width
        normed[:, lo : lo + width] = (v * inv * gain[0:1, lo : lo + width]).astype(BF)
    first = 3 - n_proj
    lane = lax.broadcasted_iota(jnp.int32, (1, PAD), 1)
    ones = jnp.where(lane == HD, 1.0, 0.0).astype(F32)
    for i in range(n_proj):
        kind = first + i
        acc = jnp.dot(normed[...], w[kind], preferred_element_type=F32)
        if kind == 0:
            acc = acc * scale
            extra = qcode[...].astype(F32)
        elif kind == 1:
            extra = kcode[...].astype(F32)
        else:
            extra = ones
        for h in range(heads):
            lo = h * PAD
            outs[i][:, lo : lo + PAD] = (acc[:, lo : lo + PAD] + extra).astype(BF)


def project(parts, gain, w, qcode, kcode, n_proj, row_start):
    rows, width = parts[0].shape
    wide = w.shape[2]
    heads = wide // PAD
    block = min(BLOCK, rows)
    steps = rows // block
    full = width * len(parts)
    first = row_start // block
    body = functools.partial(
        project_body, len(parts), n_proj, heads, HD**-0.5 * math.log2(math.e)
    )
    row = lambda i: (i, 0)
    code = pl.BlockSpec((block, PAD), lambda i: (first + i, 0))
    return pl.pallas_call(
        body,
        grid=(steps,),
        in_specs=[pl.BlockSpec((block, width), row) for _ in parts]
        + [
            pl.BlockSpec((1, full), lambda i: (0, 0)),
            pl.BlockSpec(w.shape, lambda i: (0, 0, 0), pipeline_mode=pl.Buffered(1)),
            code,
            code,
        ],
        out_specs=[pl.BlockSpec((block, wide), row) for _ in range(n_proj)],
        out_shape=[jax.ShapeDtypeStruct((rows, wide), BF) for _ in range(n_proj)],
        scratch_shapes=[pltpu.VMEM((block, full), BF)],
        compiler_params=params(24),
        cost_estimate=pl.CostEstimate(
            flops=2 * rows * full * wide * n_proj,
            bytes_accessed=2 * rows * (full + wide * n_proj) + 2 * full * wide * 3,
            transcendentals=rows,
        ),
        name="project",
    )(*parts, gain, w, qcode, kcode)


def attend_body(n_keys, heads, n_out, first_block, *refs):
    flags = refs[0]
    q = refs[1]
    keys = refs[2 : 2 + n_keys]
    vals = refs[2 + n_keys : 2 + 2 * n_keys]
    w = refs[2 + 2 * n_keys]
    outs = refs[3 + 2 * n_keys : 3 + 2 * n_keys + n_out]
    acc, top, ctx = refs[-3:]
    row_block = pl.program_id(0) + first_block
    acc[...] = jnp.zeros_like(acc)
    top[...] = jnp.full_like(top, -1e20)
    chunk = 0
    for kr, vr in zip(keys, vals):
        for lo in range(0, kr.shape[0], BLOCK):

            @pl.when(flags[row_block, chunk] > 0)
            def _(kr=kr, vr=vr, lo=lo):
                for h in range(heads):
                    c = h * PAD
                    s = lax.dot_general(
                        q[:, c : c + PAD],
                        kr[lo : lo + BLOCK, c : c + PAD],
                        (((1,), (1,)), ((), ())),
                        preferred_element_type=F32,
                    )
                    old = top[:, c : c + PAD]
                    new = jnp.maximum(old, jnp.max(s, axis=1, keepdims=True))
                    shrink = jnp.exp2(old - new)
                    wide_new = jnp.concatenate([new] * (BLOCK // PAD), axis=1)
                    p = jnp.exp2(s - wide_new).astype(BF)
                    acc[:, c : c + PAD] = acc[:, c : c + PAD] * shrink + jnp.dot(
                        p, vr[lo : lo + BLOCK, c : c + PAD], preferred_element_type=F32
                    )
                    top[:, c : c + PAD] = new

            chunk += 1
    for h in range(heads):
        c = h * PAD
        a = acc[:, c : c + PAD]
        ctx[:, c : c + PAD] = (a / a[:, HD : HD + 1]).astype(BF)
    terms = jnp.dot(ctx[...], w[...], preferred_element_type=F32)
    width = terms.shape[1] // n_out
    for k in range(n_out):
        outs[k][...] = terms[:, k * width : (k + 1) * width].astype(BF)


def attend(flags, q, keys, vals, w, n_out, first_block):
    rows, wide = q.shape
    heads = wide // PAD
    full = w.shape[1]
    n_keys = len(keys)
    kv = lambda a: pl.BlockSpec(a.shape, lambda i, f: (0, 0), pipeline_mode=pl.Buffered(1))
    key_count = sum(k.shape[0] for k in keys)
    return pl.pallas_call(
        functools.partial(attend_body, n_keys, heads, n_out, first_block),
        grid_spec=pltpu.PrefetchScalarGridSpec(
            num_scalar_prefetch=1,
            grid=(rows // BLOCK,),
            in_specs=[pl.BlockSpec((BLOCK, wide), lambda i, f: (i, 0))]
            + [kv(a) for a in keys]
            + [kv(a) for a in vals]
            + [kv(w)],
            out_specs=[
                pl.BlockSpec((BLOCK, full // n_out), lambda i, f: (i, 0)) for _ in range(n_out)
            ],
            scratch_shapes=[
                pltpu.VMEM((BLOCK, wide), F32),
                pltpu.VMEM((BLOCK, wide), F32),
                pltpu.VMEM((BLOCK, wide), BF),
            ],
        ),
        out_shape=[jax.ShapeDtypeStruct((rows, full // n_out), BF) for _ in range(n_out)],
        compiler_params=params(24),
        cost_estimate=pl.CostEstimate(
            flops=4 * rows * key_count * wide + 2 * rows * wide * full,
            bytes_accessed=2 * (rows * wide + 2 * key_count * wide + wide * full + rows * full),
            transcendentals=rows * key_count * heads,
        ),
        name="attend",
    )(flags, q, *keys, *vals, w)


def merge_body(n_out, hidden, center, inv, gain, w, *refs):
    outs = refs[:n_out]
    scaled = refs[n_out]
    values = (hidden[...].astype(F32) - center[...]) * inv[...] * gain[...]
    count = values.shape[0] // 4
    pieces = [(lo, min(PAD, values.shape[1] - lo)) for lo in range(0, values.shape[1], PAD)]
    for t, (lo, size) in enumerate(pieces):
        scaled[t, :, :size] = values[:, lo : lo + size]
    acc = None
    for j in range(4):
        rows = jnp.concatenate(
            [
                scaled.at[t][pl.ds(j, count, stride=4), :][:, :size]
                for t, (_, size) in enumerate(pieces)
            ],
            axis=1,
        ).astype(BF)
        part = jnp.dot(rows, w[j], preferred_element_type=F32)
        acc = part if acc is None else acc + part
    width = acc.shape[1] // n_out
    for k in range(n_out):
        outs[k][...] = acc[:, k * width : (k + 1) * width].astype(BF)


def merge(hidden, center, inv, gain, w, n_out):
    rows, width = hidden.shape
    full = w.shape[2]
    return pl.pallas_call(
        functools.partial(merge_body, n_out),
        out_shape=[jax.ShapeDtypeStruct((rows // 4, full // n_out), BF) for _ in range(n_out)],
        scratch_shapes=[pltpu.VMEM((pl.cdiv(width, PAD), rows, PAD), F32)],
        compiler_params=params(24),
        cost_estimate=pl.CostEstimate(
            flops=2 * rows * width * full,
            bytes_accessed=2 * (rows * width + 4 * width * full + rows * full // 4),
            transcendentals=0,
        ),
        name="merge",
    )(hidden, center, inv, gain, w)


def place_body(n_in, *refs):
    merged = sum(r[...].astype(F32) for r in refs[:n_in]).astype(BF)
    dispatch, out = refs[n_in:]
    out[...] = jnp.dot(dispatch[...], merged, preferred_element_type=F32).astype(BF)


def place(terms, dispatch):
    return pl.pallas_call(
        functools.partial(place_body, len(terms)),
        out_shape=jax.ShapeDtypeStruct((dispatch.shape[0], terms[0].shape[1]), BF),
        compiler_params=params(16),
        name="place",
    )(*terms, dispatch)


def segment_codes(ids):
    lane = jnp.arange(PAD, dtype=jnp.int32)[None, :] - HD
    used = (lane >= 0) & (lane < 2 * CODE_BITS)
    bit = (ids[:, None] >> jnp.clip(lane // 2, 0, CODE_BITS - 1)) & 1
    hit = bit == (lane & 1)
    return (
        jnp.where(used & ~hit, -FAR, 0.0).astype(BF),
        jnp.where(used & hit, 1.0, 0.0).astype(BF),
    )


def spread_square(halves):
    low, high = halves
    a0 = hop(low, "tp", 1)
    b1 = hop(high, "tp", 2)
    a1 = hop(high, "tp", 1)
    b0 = hop(low, "tp", 2)
    c = hop(a0, "tp", 2)
    d = hop(b1, "tp", 1)
    return [(low, a0, b0, c), (high, a1, b1, d)]


def shards(tokens, segment, ln_gain, w_qkv, w_out, merge_gain, w_merge, owner):
    row_count, local_width = tokens.shape
    tp_count = lax.axis_size("tp")
    grp_count = lax.axis_size("grp")
    full_width = local_width * tp_count
    heads = local_width // HD
    half = row_count // 2
    square = tp_count == 4
    me = lax.axis_index("tp")
    partner = grp_count // 2

    halves = [tokens[:half], tokens[half:]]
    far_segment = hop(segment, "grp", partner)
    far_halves = [hop(t, "grp", partner) for t in halves]
    if square:
        own_parts = spread_square(halves)
        far_parts = spread_square(far_halves)
        order = [me ^ k for k in range(4)]
    else:
        own_parts = [(lax.all_gather(t, "tp", axis=1, tiled=True),) for t in halves]
        far_parts = [(lax.all_gather(t, "tp", axis=1, tiled=True),) for t in far_halves]
        order = None

    def slices(x, axis):
        if order is None:
            return x
        return jnp.concatenate(
            [lax.dynamic_slice_in_dim(x, o * local_width, local_width, axis) for o in order],
            axis=axis,
        )

    gain = slices(ln_gain, 0)[None, :]
    w_in = slices(w_qkv, 1)
    w_in = jnp.pad(
        w_in.reshape(3, full_width, heads, HD), ((0, 0), (0, 0), (0, 0), (0, PAD - HD))
    ).reshape(3, full_width, heads * PAD)
    w_back = jnp.pad(
        slices(w_out, 1).reshape(heads, HD, full_width), ((0, 0), (0, PAD - HD), (0, 0))
    ).reshape(heads * PAD, full_width)
    w_blocks = slices(w_merge, 2)
    gain_part = lax.dynamic_slice_in_dim(merge_gain, me * local_width, local_width, 0)[None, :]

    qcode, kcode = segment_codes(segment)
    _, far_kcode = segment_codes(far_segment)
    low_ids, high_ids = segment[::BLOCK], segment[BLOCK - 1 :: BLOCK]
    key_low = jnp.concatenate([low_ids, far_segment[::BLOCK]])
    key_high = jnp.concatenate([high_ids, far_segment[BLOCK - 1 :: BLOCK]])
    flags = (
        (key_low[None, :] <= high_ids[:, None]) & (key_high[None, :] >= low_ids[:, None])
    ).astype(jnp.int32)

    merged_count = row_count // 4
    cap_slots = max(2, merged_count // grp_count * 2)
    targets = owner[:, 0]
    onehot = (targets[:, None] == jnp.arange(grp_count, dtype=jnp.int32)[None, :]).astype(F32)
    lower_mask = (
        jnp.arange(merged_count)[:, None] > jnp.arange(merged_count)[None, :]
    ).astype(F32)
    earlier = jnp.dot(lower_mask, onehot, precision=lax.Precision.HIGHEST)
    slot_index = jnp.sum(earlier * onehot, axis=1).astype(jnp.int32)
    slot_place = targets * cap_slots + slot_index
    dispatch = (
        jnp.arange(grp_count * cap_slots, dtype=jnp.int32)[:, None] == slot_place[None, :]
    ).astype(BF)

    own = [project(p, gain, w_in, qcode, kcode, 3, i * half) for i, p in enumerate(own_parts)]
    far = [
        project(p, gain, w_in, far_kcode, far_kcode, 2, i * half)
        for i, p in enumerate(far_parts)
    ]
    keys = [o[1] for o in own] + [f[0] for f in far]
    vals = [o[2] for o in own] + [f[1] for f in far]
    n_out = 4 if square else 1
    terms = [
        attend(flags, own[i][0], keys, vals, w_back, n_out, i * (half // BLOCK)) for i in range(2)
    ]

    if square:
        sums = []
        for i, (near, next_) in enumerate(((1, 2), (2, 1))):
            mine, other = terms[i][0], terms[i][next_]
            corner = hop(terms[i][3], "tp", near)
            side = hop(terms[i][near], "tp", near)
            passed = (other.astype(F32) + corner.astype(F32)).astype(BF)
            last = hop(passed, "tp", next_)
            sums.append(mine.astype(F32) + side.astype(F32) + last.astype(F32))
        summed = jnp.concatenate(sums, axis=0)
    else:
        summed = lax.psum_scatter(
            jnp.concatenate([t[0] for t in terms], axis=0),
            "tp",
            scatter_dimension=1,
            tiled=True,
        ).astype(F32)
    hidden_out = (tokens.astype(F32) + summed).astype(BF)

    local_rows = hidden_out.astype(F32)
    local_center = jnp.mean(local_rows, axis=1)
    local_spread = jnp.mean((local_rows - local_center[:, None]) ** 2, axis=1)
    stats = jnp.stack([local_center, local_spread])
    if square:
        all_stats = jnp.stack([stats] + [hop(stats, "tp", k) for k in (1, 2, 3)])
    else:
        all_stats = lax.all_gather(stats, "tp")
    center = jnp.mean(all_stats[:, 0], axis=0)
    spread = jnp.mean(all_stats[:, 1] + (all_stats[:, 0] - center[None]) ** 2, axis=0)
    inv = lax.rsqrt(spread + EPS)

    merge_terms = merge(
        hidden_out, center[:, None], inv[:, None], gain_part, w_blocks, n_out
    )
    if square:
        received = [merge_terms[0]] + [hop(merge_terms[k], "tp", k) for k in (1, 2, 3)]
    else:
        received = [lax.psum_scatter(merge_terms[0], "tp", scatter_dimension=1, tiled=True)]
    outgoing = place(received, dispatch).reshape(grp_count, cap_slots, local_width)
    routed = lax.all_to_all(outgoing, "grp", split_axis=0, concat_axis=0, tiled=True)
    return (hidden_out, routed[None])


def solution(mesh):
    return jax.shard_map(
        shards,
        mesh=mesh,
        in_specs=(
            P("grp", "tp"),
            P("grp"),
            P(),
            P(None, None, "tp"),
            P("tp", None),
            P(),
            P(None, "tp", None),
            P("grp", None),
        ),
        out_specs=(P("grp", "tp"), P("grp", None, None, "tp")),
        check_vma=False,
    )
```

```python
import functools
import math

import jax
import jax.numpy as jnp
from jax import lax
from jax.experimental import pallas as pl
from jax.experimental.pallas import tpu as pltpu
from jax.sharding import PartitionSpec as P

HD = 80
HEAD_ROWS = 96
PAD = 128
FAR = 2.0**100
EPS = 1e-06
BLOCK = 256
BF = jnp.bfloat16
F32 = jnp.float32
VM = pl.BlockSpec(memory_space=pltpu.VMEM)
SM = pl.BlockSpec(memory_space=pltpu.SMEM)


def hop(x, axis, distance):
    return lax.ppermute(x, axis, [(i, i ^ distance) for i in range(lax.axis_size(axis))])


def call(body, name, args, smem, outs, scratch, flops, transcendentals=0):
    shapes = [jax.ShapeDtypeStruct(s, d) for s, d in outs]
    size = lambda s: math.prod(s.shape) * s.dtype.itemsize
    return pl.pallas_call(
        body,
        in_specs=[SM if i < smem else VM for i in range(len(args))],
        out_specs=[VM for _ in outs],
        out_shape=shapes,
        scratch_shapes=scratch,
        compiler_params=pltpu.CompilerParams(vmem_limit_bytes=20 << 20),
        cost_estimate=pl.CostEstimate(
            flops=flops,
            bytes_accessed=sum(size(a) for a in args) + sum(size(s) for s in shapes),
            transcendentals=transcendentals,
        ),
        name=name,
    )(*args)


def project_body(n_parts, kinds, col, scale, *refs):
    order = refs[0]
    parts = refs[1 : 1 + n_parts]
    gain, w, ids = refs[1 + n_parts : 4 + n_parts]
    outs = refs[4 + n_parts : 4 + n_parts + len(kinds)]
    normed = refs[-1]
    width, rows = parts[0].shape
    heads = w.shape[1] // HD
    values = [p[...].astype(F32) for p in parts]
    center = sum(jnp.sum(v, axis=0, keepdims=True) for v in values) * (1.0 / normed.shape[0])
    values = [v - center for v in values]
    spread = sum(jnp.sum(v * v, axis=0, keepdims=True) for v in values) * (
        1.0 / normed.shape[0]
    )
    inv = lax.rsqrt(spread + EPS)
    for k, v in enumerate(values):
        at = pl.ds(pl.multiple_of(order[k] * width, 16), width)
        normed[at, :] = (v * inv * gain[at, :]).astype(BF)
    line = lax.broadcasted_iota(jnp.int32, (HEAD_ROWS - HD, rows), 0)
    bits = (jnp.broadcast_to(ids[0:1, col : col + rows], line.shape) >> (line >> 1)) & 1
    hit = bits == (line & 1)
    for kind, out in zip(kinds, outs):
        acc = jnp.dot(w[kind], normed[...], preferred_element_type=F32)
        if kind == 0:
            acc = acc * scale
            extra = jnp.where(hit, 0.0, -FAR)
        elif kind == 1:
            extra = jnp.where(hit, 1.0, 0.0)
        else:
            extra = jnp.where(line == 0, 1.0, 0.0)
        for h in range(heads):
            piece = acc[h * HD : (h + 1) * HD, :]
            if kind == 1:
                tall = jnp.concatenate(
                    [piece, extra, jnp.zeros((PAD - HEAD_ROWS, rows), F32)], axis=0
                )
                out[:, h * PAD : (h + 1) * PAD] = tall.T.astype(BF)
            else:
                lo = h * HEAD_ROWS
                out[lo : lo + HD, :] = piece.astype(BF)
                out[lo + HD : lo + HEAD_ROWS, :] = extra.astype(BF)


def project(order, parts, gain, w, ids, kinds, col):
    width, rows = parts[0].shape
    full = width * len(parts)
    heads = w.shape[1] // HD
    shape = lambda kind: (
        (rows, heads * PAD) if kind == 1 else (heads * HEAD_ROWS, rows),
        BF,
    )
    return call(
        functools.partial(
            project_body, len(parts), kinds, col, HD**-0.5 * math.log2(math.e)
        ),
        "project",
        [order, *parts, gain, w, ids],
        1,
        [shape(kind) for kind in kinds],
        [pltpu.VMEM((full, rows), BF)],
        2 * rows * full * heads * HD * len(kinds),
    )


def visit(q, kr, vr, lo, size, acc, top, cols):
    heads = q.shape[0] // HEAD_ROWS
    scores = [
        jnp.dot(
            kr[lo : lo + size, h * PAD : h * PAD + HEAD_ROWS],
            q[h * HEAD_ROWS : (h + 1) * HEAD_ROWS, :],
            preferred_element_type=F32,
        )
        for h in range(heads)
    ]
    for h, s in enumerate(scores):
        at = slice(h * HEAD_ROWS, (h + 1) * HEAD_ROWS)
        old = top[h : h + 1, cols]
        new = jnp.maximum(old, jnp.max(s, axis=0, keepdims=True))
        p = jnp.exp2(s - new).astype(BF)
        acc[at, cols] = acc[at, cols] * jnp.exp2(old - new) + jnp.dot(
            vr[at, lo : lo + size], p, preferred_element_type=F32
        )
        top[h : h + 1, cols] = new


def near_body(block, flags, q0, q1, k0, k1, v0, v1, acc, top):
    acc[...] = jnp.zeros_like(acc)
    top[...] = jnp.full_like(top, -1e20)
    sweep(block, flags, 0, (q0, q1), (k0, k1), (v0, v1), acc, top, 0)


def sweep(block, flags, first_col, qs, ks, vs, acc, top, first_q):
    per = block // BLOCK
    q_index = first_q
    col = 0
    for q in qs:
        for qc in range(0, q.shape[1], block):
            chunk = first_col
            for kr, vr in zip(ks, vs):
                for lo in range(0, kr.shape[0], BLOCK):
                    wanted = flags[q_index, chunk]
                    for extra in range(1, per):
                        wanted = wanted + flags[q_index + extra, chunk]

                    @pl.when(wanted > 0)
                    def _(q=q, qc=qc, kr=kr, vr=vr, lo=lo, col=col):
                        visit(
                            q[:, qc : qc + block], kr, vr, lo, BLOCK, acc, top,
                            slice(col, col + block),
                        )

                    chunk += 1
            q_index += per
            col += block


def near(flags, qs, ks, vs):
    wide, rows = qs[0].shape
    heads = wide // HEAD_ROWS
    return call(
        functools.partial(near_body, min(512, rows)),
        "near",
        [flags, *qs, *ks, *vs],
        1,
        [((wide, 2 * rows), F32), ((8, 2 * rows), F32)],
        [],
        16 * rows * rows * wide,
        4 * rows * rows * heads,
    )


def middle_body(flags, q0, q1, k, v, acc_in, top_in, acc, top):
    acc[...] = acc_in[...]
    top[...] = top_in[...]
    sweep(BLOCK, flags, 0, (q0, q1), (k,), (v,), acc, top, 0)


def middle(flags, qs, k, v, acc, top):
    wide, rows = qs[0].shape
    heads = wide // HEAD_ROWS
    return call(
        middle_body,
        "middle",
        [flags, *qs, k, v, acc, top],
        1,
        [(acc.shape, F32), (top.shape, F32)],
        [],
        8 * rows * rows * wide,
        2 * rows * rows * heads,
    )


def last_body(n_out, index, flags, order, q, k, v, acc_in, top_in, w, *refs):
    outs = refs[:n_out]
    acc, top, ctx = refs[n_out:]
    rows = q.shape[1]
    heads = q.shape[0] // HEAD_ROWS
    here = slice(index * rows, (index + 1) * rows)
    acc[...] = acc_in[:, here]
    top[...] = top_in[:, here]
    sweep(BLOCK, flags, k.shape[0] // BLOCK, (q,), (k,), (v,), acc, top, index * rows // BLOCK)
    for h in range(heads):
        lo = h * HEAD_ROWS
        ctx[h * HD : (h + 1) * HD, :] = (
            acc[lo : lo + HD, :] / acc[lo + HD : lo + HD + 1, :]
        ).astype(BF)
    width = outs[0].shape[0]
    for j in reversed(range(n_out)):
        at = pl.ds(pl.multiple_of(order[j] * width, 16), width)
        outs[j][...] = jnp.dot(w[at, :], ctx[...], preferred_element_type=F32).astype(BF)


def last(flags, order, q, k, v, acc, top, w, n_out, index):
    wide, rows = q.shape
    heads = wide // HEAD_ROWS
    full = w.shape[0]
    return call(
        functools.partial(last_body, n_out, index),
        "last",
        [flags, order, q, k, v, acc, top, w],
        2,
        [((full // n_out, rows), BF) for _ in range(n_out)],
        [
            pltpu.VMEM((wide, rows), F32),
            pltpu.VMEM((8, rows), F32),
            pltpu.VMEM((heads * HD, rows), BF),
        ],
        4 * rows * rows * wide + 2 * rows * heads * HD * full,
        rows * rows * heads,
    )


def hidden_body(n_half, *refs):
    hidden, stats = refs[-2:]
    inputs = refs[:-2]
    each = len(inputs) // n_half
    stats[...] = jnp.zeros_like(stats)
    for i in range(n_half):
        group = inputs[i * each : (i + 1) * each]
        rows = group[0].shape[1]
        at = slice(i * rows, (i + 1) * rows)
        total = group[0][...].astype(F32)
        for g in group[1:]:
            total = total + g[...].astype(F32)
        rounded = total.astype(BF)
        hidden[:, at] = rounded
        values = rounded.astype(F32)
        center = jnp.mean(values, axis=0, keepdims=True)
        stats[0:1, at] = center
        stats[1:2, at] = jnp.mean((values - center) ** 2, axis=0, keepdims=True)


def hidden_sum(groups):
    width, rows = groups[0][0].shape
    count = rows * len(groups)
    return call(
        functools.partial(hidden_body, len(groups)),
        "hidden",
        [x for g in groups for x in g],
        0,
        [((width, count), BF), ((8, count), F32)],
        [],
        10 * width * count,
    )


def merge_body(n_stats, n_out, order, hidden, *refs):
    stats = refs[:n_stats]
    gain, pick, w = refs[n_stats : n_stats + 3]
    outs = refs[n_stats + 3 : n_stats + 3 + n_out]
    blocks = refs[-1]
    width, rows = hidden.shape
    means = [s[0:1, :] for s in stats]
    center = sum(means) * (1.0 / n_stats)
    spread = sum(
        s[1:2, :] + (m - center) ** 2 for s, m in zip(stats, means)
    ) * (1.0 / n_stats)
    inv = lax.rsqrt(spread + EPS)
    scaled = ((hidden[...].astype(F32) - center) * inv * gain[...]).astype(BF)
    size = pick.shape[0]
    quarter = size // 4
    for lo in range(0, rows, size):
        picked = lax.dot_general(
            pick[...],
            scaled[:, lo : lo + size],
            (((1,), (1,)), ((), ())),
            preferred_element_type=F32,
        ).astype(BF)
        for j in range(4):
            blocks[lo // 4 : lo // 4 + quarter, j * width : (j + 1) * width] = picked[
                j * quarter : (j + 1) * quarter, :
            ]
    terms = jnp.dot(blocks[...], w[...], preferred_element_type=F32)
    if n_out == 1:
        outs[0][...] = terms.astype(BF)
        return
    for me in range(n_out):

        @pl.when(order[0] == me)
        def _(me=me):
            for k in range(n_out):
                lo = (me ^ k) * width
                outs[k][...] = terms[:, lo : lo + width].astype(BF)


def merge(order, hidden, stats, gain, pick, w, n_out):
    width, rows = hidden.shape
    full = w.shape[1]
    return call(
        functools.partial(merge_body, len(stats), n_out),
        "merge",
        [order, hidden, *stats, gain, pick, w],
        1,
        [((rows // 4, full // n_out), BF) for _ in range(n_out)],
        [pltpu.VMEM((rows // 4, 4 * width), BF)],
        2 * rows * width * full + 2 * rows * pick.shape[0] * width,
    )


def place_body(n_in, *refs):
    merged = sum(r[...].astype(F32) for r in refs[:n_in]).astype(BF)
    dispatch, out = refs[n_in:]
    out[...] = jnp.dot(dispatch[...], merged, preferred_element_type=F32).astype(BF)


def place(terms, dispatch):
    return call(
        functools.partial(place_body, len(terms)),
        "place",
        [*terms, dispatch],
        0,
        [((dispatch.shape[0], terms[0].shape[1]), BF)],
        [],
        2 * math.prod(dispatch.shape) * terms[0].shape[1],
    )[0]


def spread_square(halves):
    low, high = halves
    a0 = hop(low, "tp", 1)
    b1 = hop(high, "tp", 2)
    a1 = hop(high, "tp", 1)
    b0 = hop(low, "tp", 2)
    c = hop(a0, "tp", 2)
    d = hop(b1, "tp", 1)
    return [(low, a0, b0, c), (high, a1, b1, d)]


def shards(tokens, segment, ln_gain, w_qkv, w_out, merge_gain, w_merge, owner):
    row_count, local_width = tokens.shape
    tp_count = lax.axis_size("tp")
    grp_count = lax.axis_size("grp")
    full_width = local_width * tp_count
    half = row_count // 2
    square = tp_count == 4
    me = lax.axis_index("tp")
    partner = grp_count // 2
    n_out = 4 if square else 1

    tall = tokens.T
    halves = [tall[:, :half], tall[:, half:]]
    far_segment = hop(segment, "grp", partner)
    far_halves = [hop(t, "grp", partner) for t in halves]
    if square:
        own_parts = spread_square(halves)
        far_parts = spread_square(far_halves)
        order = jnp.stack([me ^ k for k in range(4)]).astype(jnp.int32)
    else:
        own_parts = [(lax.all_gather(t, "tp", axis=0, tiled=True),) for t in halves]
        far_parts = [(lax.all_gather(t, "tp", axis=0, tiled=True),) for t in far_halves]
        order = jnp.zeros((1,), jnp.int32)

    gain = ln_gain[:, None]
    w_in = jnp.swapaxes(w_qkv, 1, 2)
    w_back = w_out.T
    gain_part = lax.dynamic_slice_in_dim(merge_gain, me * local_width, local_width, 0)[:, None]
    w_blocks = w_merge.reshape(4 * local_width, full_width)

    low_ids, high_ids = segment[::BLOCK], segment[BLOCK - 1 :: BLOCK]
    meets = lambda ids: (
        (ids[::BLOCK][None, :] <= high_ids[:, None])
        & (ids[BLOCK - 1 :: BLOCK][None, :] >= low_ids[:, None])
    ).astype(jnp.int32)
    near_flags = meets(segment)
    far_flags = meets(far_segment)

    picked = jnp.arange(half, dtype=jnp.int32)
    pick = (
        (picked % (half // 4) * 4 + picked // (half // 4))[:, None] == picked[None, :]
    ).astype(BF)

    merged_count = row_count // 4
    cap_slots = max(2, merged_count // grp_count * 2)
    targets = owner[:, 0]
    onehot = (targets[:, None] == jnp.arange(grp_count, dtype=jnp.int32)[None, :]).astype(F32)
    lower_mask = (
        jnp.arange(merged_count)[:, None] > jnp.arange(merged_count)[None, :]
    ).astype(F32)
    earlier = jnp.dot(lower_mask, onehot, precision=lax.Precision.HIGHEST)
    slot_index = jnp.sum(earlier * onehot, axis=1).astype(jnp.int32)
    slot_place = targets * cap_slots + slot_index
    dispatch = (
        jnp.arange(grp_count * cap_slots, dtype=jnp.int32)[:, None] == slot_place[None, :]
    ).astype(BF)

    ids = segment[None, :]
    far_ids = far_segment[None, :]
    own = [
        project(order, p, gain, w_in, ids, (0, 1, 2), i * half) for i, p in enumerate(own_parts)
    ]
    qs, ks, vs = zip(*own)
    far = [
        project(order, p, gain, w_in, far_ids, (1, 2), i * half)
        for i, p in enumerate(far_parts)
    ]
    acc, top = near(near_flags, qs, ks, vs)
    acc, top = middle(far_flags, qs, far[0][0], far[0][1], acc, top)
    terms = [
        last(far_flags, order, qs[i], far[1][0], far[1][1], acc, top, w_back, n_out, i)
        for i in range(2)
    ]

    if square:
        groups = []
        for i, (side_hop, next_hop) in enumerate(((1, 2), (2, 1))):
            corner = hop(terms[i][3], "tp", side_hop)
            side = hop(terms[i][side_hop], "tp", side_hop)
            passed = (terms[i][next_hop].astype(F32) + corner.astype(F32)).astype(BF)
            onward = hop(passed, "tp", next_hop)
            groups.append((halves[i], terms[i][0], side, onward))
    else:
        groups = [
            (h, lax.psum_scatter(t[0], "tp", scatter_dimension=0, tiled=True))
            for h, t in zip(halves, terms)
        ]
    hidden, stats = hidden_sum(groups)
    if square:
        all_stats = [stats] + [hop(stats, "tp", k) for k in (1, 2, 3)]
    else:
        gathered = lax.all_gather(stats, "tp")
        all_stats = [gathered[k] for k in range(tp_count)]
    merge_terms = merge(order, hidden, all_stats, gain_part, pick, w_blocks, n_out)
    if square:
        received = [merge_terms[0]] + [hop(merge_terms[k], "tp", k) for k in (1, 2, 3)]
    else:
        received = [lax.psum_scatter(merge_terms[0], "tp", scatter_dimension=1, tiled=True)]
    outgoing = place(received, dispatch).reshape(grp_count, cap_slots, local_width)
    routed = lax.all_to_all(outgoing, "grp", split_axis=0, concat_axis=0, tiled=True)
    return (hidden.T, routed[None])


def solution(mesh):
    return jax.shard_map(
        shards,
        mesh=mesh,
        in_specs=(
            P("grp", "tp"),
            P("grp"),
            P(),
            P(None, None, "tp"),
            P("tp", None),
            P(),
            P(None, "tp", None),
            P("grp", None),
        ),
        out_specs=(P("grp", "tp"), P("grp", None, None, "tp")),
        check_vma=False,
    )
```

```python
import functools
import math

import jax
import jax.numpy as jnp
from jax import lax
from jax.experimental import pallas as pl
from jax.experimental.pallas import tpu as pltpu
from jax.sharding import PartitionSpec as P

HD = 80
HEAD_ROWS = 96
PAD = 128
FAR = 2.0**100
EPS = 1e-06
BLOCK = 256
BF = jnp.bfloat16
F32 = jnp.float32
VM = pl.BlockSpec(memory_space=pltpu.VMEM)
SM = pl.BlockSpec(memory_space=pltpu.SMEM)
HB = pl.BlockSpec(memory_space=pltpu.HBM)


def hop(x, axis, distance):
    return lax.ppermute(x, axis, [(i, i ^ distance) for i in range(lax.axis_size(axis))])


def nearby(count):
    if count == 1:
        return [0]
    me = lax.axis_index("tp")
    return [me ^ k for k in range(count)]


def call(body, name, args, smem, outs, scratch, loose=()):
    def place(i):
        if i < smem:
            return SM
        return HB if i in loose else VM

    return pl.pallas_call(
        body,
        in_specs=[place(i) for i in range(len(args))],
        out_specs=[VM for _ in outs],
        out_shape=[jax.ShapeDtypeStruct(s, d) for s, d in outs],
        scratch_shapes=scratch,
        compiler_params=pltpu.CompilerParams(vmem_limit_bytes=16 << 20),
        cost_estimate=pl.CostEstimate(flops=0, bytes_accessed=0, transcendentals=0),
        name=name,
    )(*args)


def prepare_body(w, gain, merge_gain, owner, w_back, gain_wide, merge_wide, dispatch):
    full = w.shape[1]
    for lo in range(0, full, PAD):
        at = slice(lo, lo + PAD)
        w_back[at, :] = w[:, at].astype(F32).T.astype(BF)
        gain_wide[at, :] = jnp.broadcast_to(gain[:, at], (PAD, PAD)).T
        merge_wide[at, :] = jnp.broadcast_to(merge_gain[:, at], (PAD, PAD)).T
    slots, count = dispatch.shape
    groups = lax.axis_size("grp")
    named = owner[...]
    onehot = jnp.broadcast_to(named, (groups, count)) == lax.broadcasted_iota(
        jnp.int32, (groups, count), 0
    )
    before = lax.broadcasted_iota(jnp.int32, (count, count), 0) < lax.broadcasted_iota(
        jnp.int32, (count, count), 1
    )
    earlier = jnp.dot(
        jnp.where(onehot, 1.0, 0.0).astype(BF),
        jnp.where(before, 1.0, 0.0).astype(BF),
        preferred_element_type=F32,
    )
    slot = jnp.sum(jnp.where(onehot, earlier, 0.0), axis=0, keepdims=True).astype(jnp.int32)
    goal = named * (slots // groups) + slot
    dispatch[...] = jnp.where(
        lax.broadcasted_iota(jnp.int32, (slots, count), 0)
        == jnp.broadcast_to(goal, (slots, count)),
        1.0,
        0.0,
    ).astype(BF)


def prepare(w, gain, merge_gain, owner, slots):
    width, full = w.shape
    count = owner.shape[0]
    return call(
        prepare_body,
        "prepare",
        [w, gain[None, :], merge_gain[None, :], owner.reshape(1, count)],
        0,
        [((full, width), BF), ((full, PAD), F32), ((full, PAD), F32), ((slots, count), BF)],
        [],
    )


def split_body(spans, source, *refs):
    outs, sem = refs[:-1], refs[-1]
    copies = [
        pltpu.make_async_copy(source.at[:, lo:hi], out, sem.at[i])
        for i, ((lo, hi), out) in enumerate(zip(spans, outs))
    ]
    for copy in copies:
        copy.start()
    for copy in copies:
        copy.wait()


def split(x, spans):
    return call(
        functools.partial(split_body, spans),
        "split",
        [x],
        0,
        [((x.shape[0], hi - lo), x.dtype) for lo, hi in spans],
        [pltpu.SemaphoreType.DMA((len(spans),))],
        loose=(0,),
    )


def project_body(places, n_parts, kinds, scale, id_start, *refs):
    count = len(places)
    sources = refs[:count]
    gain, w, ids = refs[count : 3 + count]
    outs = refs[3 + count : 3 + count + len(kinds)]
    order = nearby(n_parts)
    normed = refs[-1]
    full, rows = normed.shape
    width = full // n_parts
    heads = w.shape[0] // (3 * HD)

    def load(part, col):
        found = []
        for source, (own, _, r_lo) in zip(sources, places):
            if own == part and r_lo <= col < r_lo + source.shape[1]:
                found.append(source[:, col - r_lo : col - r_lo + PAD].astype(F32))
        return found[0] if len(found) == 1 else jnp.concatenate(found, axis=0)

    each = heads * HD
    line = lax.broadcasted_iota(jnp.int32, (HEAD_ROWS - HD, BLOCK), 0)
    for start in range(0, rows, BLOCK):
        for lo in range(start, start + BLOCK, PAD):
            here = slice(lo, lo + PAD)
            base = load(0, lo)[0:1, :]
            moved = 0.0
            square = 0.0
            for k in range(n_parts):
                off = load(k, lo) - base
                moved = moved + jnp.sum(off, axis=0, keepdims=True)
                square = square + jnp.sum(off * off, axis=0, keepdims=True)
            moved = moved * (1.0 / full)
            spread = jnp.maximum(square * (1.0 / full) - moved * moved, 0.0)
            center = base + moved
            inv = lax.rsqrt(spread + EPS)
            for k in range(n_parts):
                at = pl.ds(pl.multiple_of(order[k] * width, 16), width)
                normed[at, here] = ((load(k, lo) - center) * inv * gain[at, :]).astype(BF)
        there = slice(start, start + BLOCK)
        near_ids = ids[0:1, id_start + start : id_start + start + BLOCK]
        bits = (jnp.broadcast_to(near_ids, line.shape) >> (line >> 1)) & 1
        hit = bits == (line & 1)
        product = jnp.dot(
            w[kinds[0] * each : (kinds[-1] + 1) * each, :],
            normed[:, there],
            preferred_element_type=F32,
        )
        for i, (kind, out) in enumerate(zip(kinds, outs)):
            acc = product[i * each : (i + 1) * each, :]
            if kind == 0:
                acc = acc * scale
                extra = jnp.where(hit, 0.0, -FAR)
            elif kind == 1:
                extra = jnp.where(hit, 1.0, 0.0)
            else:
                extra = jnp.where(line == 0, 1.0, 0.0)
            for h in range(heads):
                piece = acc[h * HD : (h + 1) * HD, :]
                if kind == 1:
                    tall = jnp.concatenate(
                        [piece, extra, jnp.zeros((PAD - HEAD_ROWS, BLOCK), F32)], axis=0
                    )
                    out[there, h * PAD : (h + 1) * PAD] = tall.T.astype(BF)
                else:
                    lo = h * HEAD_ROWS
                    out[lo : lo + HD, there] = piece.astype(BF)
                    out[lo + HD : lo + HEAD_ROWS, there] = extra.astype(BF)


def project(pieces, n_parts, rows, gain, w, ids, kinds, id_start):
    full = gain.shape[0]
    heads = w.shape[0] // (3 * HD)
    shape = lambda kind: (
        (rows, heads * PAD) if kind == 1 else (heads * HEAD_ROWS, rows),
        BF,
    )
    arrays = [x for x, *_ in pieces]
    places = tuple(tuple(p[1:]) for p in pieces)
    return call(
        functools.partial(
            project_body, places, n_parts, kinds, HD**-0.5 * math.log2(math.e), id_start
        ),
        "project",
        [*arrays, gain, w, ids],
        0,
        [shape(kind) for kind in kinds],
        [pltpu.VMEM((full, rows), BF)],
    )


def visit(q, kr, vr, lo, size, acc, top, cols):
    heads = q.shape[0] // HEAD_ROWS
    scores = [
        jnp.dot(
            kr[lo : lo + size, h * PAD : h * PAD + HEAD_ROWS],
            q[h * HEAD_ROWS : (h + 1) * HEAD_ROWS, :],
            preferred_element_type=F32,
        )
        for h in range(heads)
    ]
    for h, s in enumerate(scores):
        at = slice(h * HEAD_ROWS, (h + 1) * HEAD_ROWS)
        old = top[h : h + 1, cols]
        new = jnp.maximum(old, jnp.max(s, axis=0, keepdims=True))
        p = jnp.exp2(s - new).astype(BF)
        acc[at, cols] = acc[at, cols] * jnp.exp2(old - new) + jnp.dot(
            vr[at, lo : lo + size], p, preferred_element_type=F32
        )
        top[h : h + 1, cols] = new


def sweep(block, q_ids, k_ids, k_start, q, q_start, kr, vr, acc, top):
    for col in range(0, acc.shape[1], block):
        row = q_start + col
        for lo in range(0, kr.shape[0], BLOCK):
            meets = (k_ids[k_start + lo] <= q_ids[row + block - 1]) & (
                k_ids[k_start + lo + BLOCK - 1] >= q_ids[row]
            )

            @pl.when(meets)
            def _(col=col, row=row, lo=lo):
                visit(
                    q[:, row : row + block], kr, vr, lo, BLOCK, acc, top,
                    slice(col, col + block),
                )


def near_body(block, q_ids, q, k, v, acc, top):
    acc[...] = jnp.zeros_like(acc)
    top[...] = jnp.full_like(top, -1e20)
    sweep(block, q_ids, q_ids, 0, q, 0, k, v, acc, top)


def near(q_ids, q, k, v):
    wide, rows = q.shape
    heads = wide // HEAD_ROWS
    return call(
        functools.partial(near_body, 2 * BLOCK),
        "near",
        [q_ids, q, k, v],
        1,
        [((wide, rows), F32), ((8, rows), F32)],
        [],
    )


def middle_body(start, q_ids, k_ids, q, k, v, acc_in, top_in, acc, top):
    acc[...] = acc_in[...]
    top[...] = top_in[...]
    sweep(BLOCK, q_ids, k_ids, start, q, 0, k, v, acc, top)


def middle(q_ids, k_ids, q, k, v, acc, top, start):
    wide, rows = q.shape
    heads = wide // HEAD_ROWS
    return call(
        functools.partial(middle_body, start),
        "middle",
        [q_ids, k_ids, q, k, v, acc, top],
        2,
        [(acc.shape, F32), (top.shape, F32)],
        [],
    )


def last_body(n_out, start, k_start, q_ids, k_ids, q, k, v, acc_in, top_in, w, *refs):
    outs = refs[:n_out]
    acc, top, ctx = refs[n_out:]
    rows = acc.shape[1]
    heads = q.shape[0] // HEAD_ROWS
    acc[...] = acc_in[:, start : start + rows]
    top[...] = top_in[:, start : start + rows]
    sweep(BLOCK, q_ids, k_ids, k_start, q, start, k, v, acc, top)
    for h in range(heads):
        lo = h * HEAD_ROWS
        ctx[h * HD : (h + 1) * HD, :] = (
            acc[lo : lo + HD, :] / acc[lo + HD : lo + HD + 1, :]
        ).astype(BF)
    width = outs[0].shape[0]
    order = nearby(n_out)
    for j in reversed(range(n_out)):
        at = pl.ds(pl.multiple_of(order[j] * width, 16), width)
        outs[j][...] = jnp.dot(w[at, :], ctx[...], preferred_element_type=F32).astype(BF)


def last(q_ids, k_ids, q, k, v, acc, top, w, n_out, start, rows, k_start):
    wide = q.shape[0]
    heads = wide // HEAD_ROWS
    full = w.shape[0]
    return call(
        functools.partial(last_body, n_out, start, k_start),
        "last",
        [q_ids, k_ids, q, k, v, acc, top, w],
        2,
        [((full // n_out, rows), BF) for _ in range(n_out)],
        [
            pltpu.VMEM((wide, rows), F32),
            pltpu.VMEM((8, rows), F32),
            pltpu.VMEM((heads * HD, rows), BF),
        ],
    )


def hidden_body(n_half, tokens, *refs):
    hidden, again, stats = refs[-3:]
    inputs = refs[:-3]
    each = len(inputs) // n_half
    rows = hidden.shape[1] // n_half
    for i in range(n_half):
        for lo in range(0, rows, PAD):
            at = slice(i * rows + lo, i * rows + lo + PAD)
            total = tokens[:, at].astype(F32)
            for g in inputs[i * each : (i + 1) * each]:
                total = total + g[:, lo : lo + PAD].astype(F32)
            rounded = total.astype(BF)
            hidden[:, at] = rounded
            again[:, at] = rounded
            values = rounded.astype(F32)
            center = jnp.mean(values, axis=0, keepdims=True)
            spread = jnp.mean((values - center) ** 2, axis=0, keepdims=True)
            stats[:, at] = jnp.concatenate(
                [center, spread, jnp.zeros((6, PAD), F32)], axis=0
            )


def hidden_sum(tokens, groups):
    width, count = tokens.shape
    return call(
        functools.partial(hidden_body, len(groups)),
        "hidden",
        [tokens, *[x for g in groups for x in g]],
        0,
        [((width, count), BF), ((width, count), BF), ((8, count), F32)],
        [],
    )


def merge_body(n_stats, n_out, source, *refs):
    stats = refs[:n_stats]
    gain, w = refs[n_stats : n_stats + 2]
    outs = refs[n_stats + 2 : n_stats + 2 + n_out]
    scaled, blocks, pick = refs[-3:]
    width, rows = source.shape
    me = lax.axis_index("tp")
    own_gain = gain[pl.ds(pl.multiple_of(me * width, 16), width), :]
    row = lax.broadcasted_iota(jnp.int32, pick.shape, 0)
    col = lax.broadcasted_iota(jnp.int32, pick.shape, 1)
    fourth = pick.shape[0] // 4
    pick[...] = jnp.where(4 * (row % fourth) + row // fourth == col, 1.0, 0.0).astype(BF)
    for lo in range(0, rows, PAD):
        at = slice(lo, lo + PAD)
        means = [s[0:1, at] for s in stats]
        center = sum(means) * (1.0 / n_stats)
        spread = sum(
            s[1:2, at] + (m - center) ** 2 for s, m in zip(stats, means)
        ) * (1.0 / n_stats)
        inv = lax.rsqrt(spread + EPS)
        scaled[:, at] = ((source[:, at].astype(F32) - center) * inv * own_gain).astype(BF)
    size = pick.shape[0]
    quarter = size // 4
    for lo in range(0, rows, size):
        picked = lax.dot_general(
            pick[...],
            scaled[:, lo : lo + size],
            (((1,), (1,)), ((), ())),
            preferred_element_type=F32,
        ).astype(BF)
        for j in range(4):
            blocks[lo // 4 : lo // 4 + quarter, j * width : (j + 1) * width] = picked[
                j * quarter : (j + 1) * quarter, :
            ]
    terms = jnp.dot(blocks[...], w[...], preferred_element_type=F32)
    if n_out == 1:
        outs[0][...] = terms.astype(BF)
        return
    for case in range(n_out):

        @pl.when(me == case)
        def _(case=case):
            for k in range(n_out):
                lo = (case ^ k) * width
                outs[k][...] = terms[:, lo : lo + width].astype(BF)


def merge(hidden, stats, gain, w, n_out):
    width, rows = hidden.shape
    full = w.shape[1]
    return call(
        functools.partial(merge_body, len(stats), n_out),
        "merge",
        [hidden, *stats, gain, w],
        0,
        [((rows // 4, full // n_out), BF) for _ in range(n_out)],
        [
            pltpu.VMEM((width, rows), BF),
            pltpu.VMEM((rows // 4, 4 * width), BF),
            pltpu.VMEM((rows // 2, rows // 2), BF),
        ],
    )


def place_body(n_in, crossing, *refs):
    merged = sum(r[...].astype(F32) for r in refs[:n_in]).astype(BF)
    dispatch = refs[n_in]
    placed = jnp.dot(dispatch[...], merged, preferred_element_type=F32).astype(BF)
    if not crossing:
        refs[-1][...] = placed
        return
    whole = refs[-1]
    whole[...] = placed
    group = lax.axis_index("grp")
    for k, out in enumerate(refs[n_in + 1 : -1]):
        cap = out.shape[0] // 2
        for e in range(2):
            at = pl.ds(pl.multiple_of((group ^ (2 * k + e)) * cap, 16), cap)
            out[e * cap : (e + 1) * cap, :] = whole[at, :]


def place(terms, dispatch, n_out):
    slots = dispatch.shape[0]
    width = terms[0].shape[1]
    return call(
        functools.partial(place_body, len(terms), n_out > 1),
        "place",
        [*terms, dispatch],
        0,
        [((slots // n_out, width), BF) for _ in range(n_out)],
        [pltpu.VMEM((slots, width), BF)] if n_out > 1 else [],
    )


def settle_body(*refs):
    crossed, out = refs[-2:]
    cap = out.shape[1]
    group = lax.axis_index("grp")
    for k, block in enumerate(refs[:-2]):
        out[pl.ds(group ^ (2 * k), 1)] = block[:cap, :][None]
        out[pl.ds(group ^ (2 * k + 1), 1)] = crossed[k * cap : (k + 1) * cap, :][None]


def settle(blocks, crossed, cap):
    width = crossed.shape[1]
    return call(
        settle_body,
        "settle",
        [*blocks, crossed],
        0,
        [((2 * len(blocks), cap, width), BF)],
        [],
    )[0]


def shards(tokens, segment, ln_gain, w_qkv, w_out, merge_gain, w_merge, owner):
    row_count, local_width = tokens.shape
    tp_count = lax.axis_size("tp")
    grp_count = lax.axis_size("grp")
    full_width = local_width * tp_count
    half = row_count // 2
    square = tp_count == 4
    partner = grp_count // 2
    n_out = 4 if square else 1
    after = lambda x, *first: lax.optimization_barrier((x, *first))[0]

    tall = tokens.T
    spans = ((0, half), (half, row_count))
    far_segment = hop(segment, "grp", partner)
    merged_count = row_count // 4
    cap_slots = max(2, merged_count // grp_count * 2)
    w_back, gain, merge_wide, dispatch = prepare(
        w_out, ln_gain, merge_gain, owner, grp_count * cap_slots
    )
    w_in = jnp.swapaxes(w_qkv, 1, 2).reshape(3 * local_width, full_width)
    w_blocks = w_merge.reshape(4 * local_width, full_width)

    def keys_of(pieces, start):
        return project(pieces, n_out, half, gain, w_in, far_segment[None, :], (1, 2), start)

    def own_of(pieces):
        return project(
            pieces, n_out, row_count, gain, w_in, segment[None, :], (0, 1, 2), 0
        )

    if square:
        mid = local_width // 2
        a = hop(tall, "tp", 1)
        b = hop(tall, "tp", 2)
        h0, h1 = split(tall, spans)
        z0 = hop(h0, "grp", partner)
        c = hop(after(a, w_back)[:mid], "tp", 2)
        d = hop(b[mid:], "tp", 1)
        z1 = hop(after(h1, z0), "grp", partner)
        q, k, v = own_of(
            [(tall, 0, 0, 0), (a, 1, 0, 0), (b, 2, 0, 0), (c, 3, 0, 0), (d, 3, mid, 0)]
        )
        z0 = after(z0, c, d)
        za0 = hop(z0, "tp", 1)
        zb0 = hop(z0, "tp", 2)
        z1 = after(z1, k, za0, zb0)
        za1 = hop(z1, "tp", 1)
        zb1 = hop(z1, "tp", 2)
        ta0, tb0 = za0[:mid], zb0[mid:]
        zc0 = hop(ta0, "tp", 2)
        zd0 = hop(tb0, "tp", 1)
        acc, top = near(segment, after(q, z1, ta0, tb0), k, v)
        za1, zb1, far_segment = lax.optimization_barrier((za1, zb1, far_segment, top))[:3]
        ta1, tb1 = za1[:mid], zb1[mid:]
        zc1 = hop(ta1, "tp", 2)
        zd1 = hop(tb1, "tp", 1)
        far0 = keys_of(
            [(z0, 0, 0, 0), (za0, 1, 0, 0), (zb0, 2, 0, 0), (zc0, 3, 0, 0), (zd0, 3, mid, 0)],
            0,
        )
        acc, top = middle(segment, far_segment, q, *far0, acc, top, 0)
        far1 = keys_of(
            [(z1, 0, 0, 0), (za1, 1, 0, 0), (zb1, 2, 0, 0), (zc1, 3, 0, 0), (zd1, 3, mid, 0)],
            half,
        )
    else:
        q, k, v = own_of([(lax.all_gather(tall, "tp", axis=0, tiled=True), 0, 0, 0)])
        far_whole = lax.all_gather(hop(tall, "grp", partner), "tp", axis=0, tiled=True)
        far0, far1 = [keys_of([(far_whole[:, lo:hi], 0, 0, 0)], lo) for lo, hi in spans]
        acc, top = near(segment, q, k, v)
        acc, top = middle(segment, far_segment, q, *far0, acc, top, 0)

    crossing = grp_count == 8
    terms = [
        last(segment, far_segment, q, *far1, acc, top, w_back, n_out, start, half, half)
        for start in (0, half)
    ]

    if square:
        groups = []
        for i, (side_hop, next_hop) in enumerate(((1, 2), (2, 1))):
            corner = hop(terms[i][3], "tp", side_hop)
            side = hop(terms[i][side_hop], "tp", side_hop)
            passed = (terms[i][next_hop].astype(F32) + corner.astype(F32)).astype(BF)
            onward = hop(passed, "tp", next_hop)
            groups.append((terms[i][0], side, onward))
    else:
        groups = [
            (lax.psum_scatter(t[0], "tp", scatter_dimension=0, tiled=True),) for t in terms
        ]
    hidden_out, hidden, stats = hidden_sum(tall, groups)
    if square:
        all_stats = [stats] + [hop(stats, "tp", n) for n in (1, 2, 3)]
    else:
        gathered = lax.all_gather(stats, "tp")
        all_stats = [gathered[n] for n in range(tp_count)]
    merge_terms = merge(hidden, all_stats, merge_wide, w_blocks, n_out)
    if square:
        received = [merge_terms[0]] + [hop(merge_terms[n], "tp", n) for n in (1, 2, 3)]
    else:
        received = [lax.psum_scatter(merge_terms[0], "tp", scatter_dimension=1, tiled=True)]
    if crossing:
        blocks = place(received, dispatch, grp_count // 2)
        blocks = [blocks[0]] + [
            hop(block, "grp", 2 * n) for n, block in enumerate(blocks) if n > 0
        ]
        crossed = hop(
            jnp.concatenate([block[cap_slots:] for block in blocks], axis=0), "grp", 1
        )
        routed = settle(blocks, crossed, cap_slots)
    else:
        outgoing = place(received, dispatch, 1)[0].reshape(grp_count, cap_slots, local_width)
        routed = lax.all_to_all(outgoing, "grp", split_axis=0, concat_axis=0, tiled=True)
    return (hidden_out.T, routed[None])


def solution(mesh):
    return jax.shard_map(
        shards,
        mesh=mesh,
        in_specs=(
            P("grp", "tp"),
            P("grp"),
            P(),
            P(None, None, "tp"),
            P("tp", None),
            P(),
            P(None, "tp", None),
            P("grp", None),
        ),
        out_specs=(P("grp", "tp"), P("grp", None, None, "tp")),
        check_vma=False,
    )
```

```python
import functools
import math

import jax
import jax.numpy as jnp
from jax import lax
from jax.experimental import pallas as pl
from jax.experimental.pallas import tpu as pltpu
from jax.sharding import PartitionSpec as P

HD = 80
HEAD_ROWS = 96
PAD = 128
FAR = 2.0**100
EPS = 1e-06
BLOCK = 256
BF = jnp.bfloat16
F32 = jnp.float32
VM = pl.BlockSpec(memory_space=pltpu.VMEM)
SM = pl.BlockSpec(memory_space=pltpu.SMEM)
HB = pl.BlockSpec(memory_space=pltpu.HBM)


def hop(x, axis, distance):
    return lax.ppermute(x, axis, [(i, i ^ distance) for i in range(lax.axis_size(axis))])


def nearby(count):
    if count == 1:
        return [0]
    me = lax.axis_index("tp")
    return [me ^ k for k in range(count)]


def call(body, name, args, smem, outs, scratch, loose=()):
    def place(i):
        if i < smem:
            return SM
        return HB if i in loose else VM

    return pl.pallas_call(
        body,
        in_specs=[place(i) for i in range(len(args))],
        out_specs=[VM for _ in outs],
        out_shape=[jax.ShapeDtypeStruct(s, d) for s, d in outs],
        scratch_shapes=scratch,
        compiler_params=pltpu.CompilerParams(vmem_limit_bytes=16 << 20),
        cost_estimate=pl.CostEstimate(flops=0, bytes_accessed=0, transcendentals=0),
        name=name,
    )(*args)


def prepare_body(
    crossing, w, w_merge, gain, merge_gain, owner, ids, *outs
):
    w_back, w_tall, gain_wide, merge_wide, dispatch, ids_row = outs
    ids_row[...] = ids[...]
    full = w.shape[1]
    for lo in range(0, full, PAD):
        at = slice(lo, lo + PAD)
        w_back[at, :] = w[:, at].astype(F32).T.astype(BF)
        gain_wide[at, :] = jnp.broadcast_to(gain[:, at], (PAD, PAD)).T
        merge_wide[at, :] = jnp.broadcast_to(merge_gain[:, at], (PAD, PAD)).T
        for low in range(0, w_merge.shape[0], 4 * PAD):
            high = min(low + 4 * PAD, w_merge.shape[0])
            w_tall[at, low:high] = w_merge[low:high, at].astype(F32).T.astype(BF)
    slots, count = dispatch.shape
    groups = lax.axis_size("grp")
    named = owner[...]
    if crossing:
        named = named ^ lax.axis_index("grp")
    onehot = jnp.broadcast_to(named, (groups, count)) == lax.broadcasted_iota(
        jnp.int32, (groups, count), 0
    )
    before = lax.broadcasted_iota(jnp.int32, (count, count), 0) < lax.broadcasted_iota(
        jnp.int32, (count, count), 1
    )
    earlier = jnp.dot(
        jnp.where(onehot, 1.0, 0.0).astype(BF),
        jnp.where(before, 1.0, 0.0).astype(BF),
        preferred_element_type=F32,
    )
    slot = jnp.sum(jnp.where(onehot, earlier, 0.0), axis=0, keepdims=True).astype(jnp.int32)
    goal = named * (slots // groups) + slot
    dispatch[...] = jnp.where(
        lax.broadcasted_iota(jnp.int32, (slots, count), 0)
        == jnp.broadcast_to(goal, (slots, count)),
        1.0,
        0.0,
    ).astype(BF)


def prepare(w, w_merge, gain, merge_gain, owner, ids, slots, crossing):
    width, full = w.shape
    count = owner.shape[0]
    return call(
        functools.partial(prepare_body, crossing),
        "prepare",
        [w, w_merge, gain[None, :], merge_gain[None, :], owner.reshape(1, count), ids],
        0,
        [
            ((full, width), BF),
            (w_merge.shape[::-1], BF),
            ((full, PAD), F32),
            ((full, PAD), F32),
            ((slots, count), BF),
            (ids.shape, jnp.int32),
        ],
        [],
    )


def split_body(spans, source, *refs):
    outs, sem = refs[:-1], refs[-1]
    copies = [
        pltpu.make_async_copy(source.at[:, lo:hi], out, sem.at[i])
        for i, ((lo, hi), out) in enumerate(zip(spans, outs))
    ]
    for copy in copies:
        copy.start()
    for copy in copies:
        copy.wait()


def split(x, spans):
    return call(
        functools.partial(split_body, spans),
        "split",
        [x],
        0,
        [((x.shape[0], hi - lo), x.dtype) for lo, hi in spans],
        [pltpu.SemaphoreType.DMA((len(spans),))],
        loose=(0,),
    )


def project_body(places, n_parts, kinds, scale, id_start, *refs):
    count = len(places)
    sources = refs[:count]
    gain, w, ids = refs[count : 3 + count]
    outs = refs[3 + count : 3 + count + len(kinds)]
    order = nearby(n_parts)
    normed = refs[-1]
    full, rows = normed.shape
    width = full // n_parts
    heads = w.shape[0] // (3 * HD)

    def load(part, col):
        found = []
        for source, (own, _, r_lo) in zip(sources, places):
            if own == part and r_lo <= col < r_lo + source.shape[1]:
                found.append(source[:, col - r_lo : col - r_lo + PAD].astype(F32))
        return found[0] if len(found) == 1 else jnp.concatenate(found, axis=0)

    each = heads * HD
    line = lax.broadcasted_iota(jnp.int32, (HEAD_ROWS - HD, BLOCK), 0)
    for start in range(0, rows, BLOCK):
        for lo in range(start, start + BLOCK, PAD):
            here = slice(lo, lo + PAD)
            base = load(0, lo)[0:1, :]
            moved = 0.0
            square = 0.0
            for k in range(n_parts):
                off = load(k, lo) - base
                moved = moved + jnp.sum(off, axis=0, keepdims=True)
                square = square + jnp.sum(off * off, axis=0, keepdims=True)
            moved = moved * (1.0 / full)
            spread = jnp.maximum(square * (1.0 / full) - moved * moved, 0.0)
            center = base + moved
            inv = lax.rsqrt(spread + EPS)
            for k in range(n_parts):
                at = pl.ds(pl.multiple_of(order[k] * width, 16), width)
                normed[at, here] = ((load(k, lo) - center) * inv * gain[at, :]).astype(BF)
        there = slice(start, start + BLOCK)
        near_ids = ids[0:1, id_start + start : id_start + start + BLOCK]
        bits = (jnp.broadcast_to(near_ids, line.shape) >> (line >> 1)) & 1
        hit = bits == (line & 1)
        product = jnp.dot(
            w[kinds[0] * each : (kinds[-1] + 1) * each, :],
            normed[:, there],
            preferred_element_type=F32,
        )
        for i, (kind, out) in enumerate(zip(kinds, outs)):
            acc = product[i * each : (i + 1) * each, :]
            if kind == 0:
                acc = acc * scale
                extra = jnp.where(hit, 0.0, -FAR)
            elif kind == 1:
                extra = jnp.where(hit, 1.0, 0.0)
            else:
                extra = jnp.where(line == 0, 1.0, 0.0)
            for h in range(heads):
                piece = acc[h * HD : (h + 1) * HD, :]
                if kind == 1:
                    tall = jnp.concatenate(
                        [piece, extra, jnp.zeros((PAD - HEAD_ROWS, BLOCK), F32)], axis=0
                    )
                    out[there, h * PAD : (h + 1) * PAD] = tall.T.astype(BF)
                else:
                    lo = h * HEAD_ROWS
                    out[lo : lo + HD, there] = piece.astype(BF)
                    out[lo + HD : lo + HEAD_ROWS, there] = extra.astype(BF)


def project(pieces, n_parts, rows, gain, w, ids, kinds, id_start):
    full = gain.shape[0]
    heads = w.shape[0] // (3 * HD)
    shape = lambda kind: (
        (rows, heads * PAD) if kind == 1 else (heads * HEAD_ROWS, rows),
        BF,
    )
    arrays = [x for x, *_ in pieces]
    places = tuple(tuple(p[1:]) for p in pieces)
    return call(
        functools.partial(
            project_body, places, n_parts, kinds, HD**-0.5 * math.log2(math.e), id_start
        ),
        "project",
        [*arrays, gain, w, ids],
        0,
        [shape(kind) for kind in kinds],
        [pltpu.VMEM((full, rows), BF)],
    )


def visit(q, kr, vr, lo, size, acc, top, cols):
    heads = q.shape[0] // HEAD_ROWS
    scores = [
        jnp.dot(
            kr[lo : lo + size, h * PAD : h * PAD + HEAD_ROWS],
            q[h * HEAD_ROWS : (h + 1) * HEAD_ROWS, :],
            preferred_element_type=F32,
        )
        for h in range(heads)
    ]
    for h, s in enumerate(scores):
        at = slice(h * HEAD_ROWS, (h + 1) * HEAD_ROWS)
        old = top[h : h + 1, cols]
        new = jnp.maximum(old, jnp.max(s, axis=0, keepdims=True))
        p = jnp.exp2(s - new).astype(BF)
        acc[at, cols] = acc[at, cols] * jnp.exp2(old - new) + jnp.dot(
            vr[at, lo : lo + size], p, preferred_element_type=F32
        )
        top[h : h + 1, cols] = new


def sweep(block, q_ids, k_ids, k_start, q, q_start, kr, vr, acc, top):
    for col in range(0, acc.shape[1], block):
        row = q_start + col
        for lo in range(0, kr.shape[0], BLOCK):
            meets = (k_ids[k_start + lo] <= q_ids[row + block - 1]) & (
                k_ids[k_start + lo + BLOCK - 1] >= q_ids[row]
            )

            @pl.when(meets)
            def _(col=col, row=row, lo=lo):
                visit(
                    q[:, row : row + block], kr, vr, lo, BLOCK, acc, top,
                    slice(col, col + block),
                )


def near_body(block, q_ids, q, k, v, *refs):
    for i in range(0, len(refs), 2):
        acc, top = refs[i : i + 2]
        acc[...] = jnp.zeros_like(acc)
        top[...] = jnp.full_like(top, -1e20)
        sweep(block, q_ids, q_ids, 0, q, i // 2 * acc.shape[1], k, v, acc, top)


def near(q_ids, q, k, v):
    wide, rows = q.shape
    a0, t0, a1, t1 = call(
        functools.partial(near_body, 2 * BLOCK),
        "near",
        [q_ids, q, k, v],
        1,
        [((wide, rows // 2), F32), ((8, rows // 2), F32)] * 2,
        [],
    )
    return [(a0, t0), (a1, t1)]


def middle_body(k_start, q_ids, k_ids, q, k, v, *refs):
    count = len(refs) // 4
    for i in range(count):
        acc_in, top_in = refs[2 * i : 2 * i + 2]
        acc, top = refs[2 * (count + i) : 2 * (count + i) + 2]
        acc[...] = acc_in[...]
        top[...] = top_in[...]
        sweep(BLOCK, q_ids, k_ids, k_start, q, i * acc.shape[1], k, v, acc, top)


def middle(q_ids, k_ids, q, k, v, states, k_start):
    flat = [x for state in states for x in state]
    found = call(
        functools.partial(middle_body, k_start),
        "middle",
        [q_ids, k_ids, q, k, v, *flat],
        2,
        [(x.shape, F32) for x in flat],
        [],
    )
    return [tuple(found[2 * i : 2 * i + 2]) for i in range(len(states))]


def multiply(w, index, width, ctx):
    at = pl.ds(pl.multiple_of(index * width, 16), width)
    return jnp.dot(w[at, :], ctx, preferred_element_type=F32).astype(BF)


def last_body(count, n_out, k_start, q_ids, k_ids, q, k, v, w, *refs):
    states = refs[: 2 * count]
    ctx = refs[2 * count]
    outs = refs[2 * count + 1 : 3 * count + 1]
    acc, top = refs[3 * count + 1 :]
    rows = acc.shape[1]
    heads = q.shape[0] // HEAD_ROWS
    order = nearby(n_out)
    for i in range(count):
        at = slice(i * rows, (i + 1) * rows)
        acc[...] = states[2 * i][...]
        top[...] = states[2 * i + 1][...]
        sweep(BLOCK, q_ids, k_ids, k_start, q, i * rows, k, v, acc, top)
        for h in range(heads):
            lo = h * HEAD_ROWS
            ctx[h * HD : (h + 1) * HD, at] = (
                acc[lo : lo + HD, :] / acc[lo + HD : lo + HD + 1, :]
            ).astype(BF)
        outs[i][...] = multiply(w, order[-1], outs[i].shape[0], ctx[:, at])


def last(q_ids, k_ids, q, k, v, states, w, n_out, k_start):
    wide, rows = q.shape
    count = len(states)
    part = rows // count
    return call(
        functools.partial(last_body, count, n_out, k_start),
        "last",
        [q_ids, k_ids, q, k, v, w, *[x for state in states for x in state]],
        2,
        [((w.shape[1], rows), BF)] + [((w.shape[0] // n_out, part), BF) for _ in states],
        [pltpu.VMEM((wide, part), F32), pltpu.VMEM((8, part), F32)],
    )


def rest_body(n_out, ctx, w, *outs):
    order = nearby(n_out)
    count = len(outs) // (n_out - 1)
    rows = ctx.shape[1] // count
    for j in range(n_out - 1):
        found = multiply(w, order[j], outs[0].shape[0], ctx[...])
        for i in range(count):
            outs[j * count + i][...] = found[:, i * rows : (i + 1) * rows]


def rest(ctx, w, n_out, count):
    found = call(
        functools.partial(rest_body, n_out),
        "rest",
        [ctx, w],
        0,
        [
            ((w.shape[0] // n_out, ctx.shape[1] // count), BF)
            for _ in range((n_out - 1) * count)
        ],
        [],
    )
    return [[found[j * count + i] for j in range(n_out - 1)] for i in range(count)]


def hidden_body(n_half, *refs):
    hidden, again, stats = refs[-3:]
    inputs = refs[:-3]
    each = len(inputs) // n_half
    rows = hidden.shape[1] // n_half
    for i in range(n_half):
        for lo in range(0, rows, PAD):
            at = slice(i * rows + lo, i * rows + lo + PAD)
            total = 0.0
            for g in inputs[i * each : (i + 1) * each]:
                total = total + g[:, lo : lo + PAD].astype(F32)
            rounded = total.astype(BF)
            hidden[:, at] = rounded
            again[:, at] = rounded
            values = rounded.astype(F32)
            center = jnp.mean(values, axis=0, keepdims=True)
            spread = jnp.mean((values - center) ** 2, axis=0, keepdims=True)
            stats[:, at] = jnp.concatenate(
                [center, spread, jnp.zeros((6, PAD), F32)], axis=0
            )


def hidden_sum(groups):
    width, rows = groups[0][0].shape
    count = rows * len(groups)
    return call(
        functools.partial(hidden_body, len(groups)),
        "hidden",
        [x for g in groups for x in g],
        0,
        [((width, count), BF), ((width, count), BF), ((8, count), F32)],
        [],
    )


def merge_body(n_stats, n_out, source, *refs):
    stats = refs[:n_stats]
    gain, w = refs[n_stats : n_stats + 2]
    outs = refs[n_stats + 2 : n_stats + 2 + n_out]
    scaled, blocks, pick = refs[-3:]
    width, rows = source.shape
    me = lax.axis_index("tp")
    own_gain = gain[pl.ds(pl.multiple_of(me * width, 16), width), :]
    row = lax.broadcasted_iota(jnp.int32, pick.shape, 0)
    col = lax.broadcasted_iota(jnp.int32, pick.shape, 1)
    fourth = pick.shape[0] // 4
    pick[...] = jnp.where(4 * (row % fourth) + row // fourth == col, 1.0, 0.0).astype(BF)
    for lo in range(0, rows, PAD):
        at = slice(lo, lo + PAD)
        means = [s[0:1, at] for s in stats]
        center = sum(means) * (1.0 / n_stats)
        spread = sum(
            s[1:2, at] + (m - center) ** 2 for s, m in zip(stats, means)
        ) * (1.0 / n_stats)
        inv = lax.rsqrt(spread + EPS)
        scaled[:, at] = ((source[:, at].astype(F32) - center) * inv * own_gain).astype(BF)
    size = pick.shape[0]
    quarter = size // 4
    for lo in range(0, rows, size):
        picked = lax.dot_general(
            pick[...],
            scaled[:, lo : lo + size],
            (((1,), (1,)), ((), ())),
            preferred_element_type=F32,
        ).astype(BF)
        for j in range(4):
            blocks[lo // 4 : lo // 4 + quarter, j * width : (j + 1) * width] = picked[
                j * quarter : (j + 1) * quarter, :
            ]
    order = nearby(n_out)
    for j in range(n_out):
        tall = outs[j].shape[0]
        at = pl.ds(pl.multiple_of(order[j] * tall, 16), tall)
        outs[j][...] = lax.dot_general(
            w[at, :], blocks[...], (((1,), (1,)), ((), ())), preferred_element_type=F32
        ).astype(BF)


def merge(hidden, stats, gain, w, n_out):
    width, rows = hidden.shape
    full = w.shape[0]
    return call(
        functools.partial(merge_body, len(stats), n_out),
        "merge",
        [hidden, *stats, gain, w],
        0,
        [((full // n_out, rows // 4), BF) for _ in range(n_out)],
        [
            pltpu.VMEM((width, rows), BF),
            pltpu.VMEM((rows // 4, 4 * width), BF),
            pltpu.VMEM((rows // 2, rows // 2), BF),
        ],
    )


def place_body(n_in, *refs):
    merged = sum(r[...].astype(F32) for r in refs[:n_in]).astype(BF)
    dispatch = refs[n_in]
    outs = refs[n_in + 1 :]
    dims = (((1,), (1,)), ((), ()))
    if len(outs) == 1:
        outs[0][...] = lax.dot_general(
            dispatch[...], merged, dims, preferred_element_type=F32
        ).astype(BF)
        return
    placed = lax.dot_general(merged, dispatch[...], dims, preferred_element_type=F32)
    for k, out in enumerate(outs):
        size = out.shape[1]
        out[...] = placed[:, k * size : (k + 1) * size].astype(BF)


def place(terms, dispatch, n_out):
    slots = dispatch.shape[0]
    width = terms[0].shape[0]
    return call(
        functools.partial(place_body, len(terms)),
        "place",
        [*terms, dispatch],
        0,
        [((width, slots // n_out) if n_out > 1 else (slots, width), BF) for _ in range(n_out)],
        [],
    )


def gather_body(*refs):
    out = refs[-1]
    cap = out.shape[1] // (len(refs) - 1)
    for k, block in enumerate(refs[:-1]):
        out[:, k * cap : (k + 1) * cap] = block[:, cap:]


def settle_body(*refs):
    crossed, out = refs[-2:]
    cap = out.shape[1]
    group = lax.axis_index("grp")
    for k, block in enumerate(refs[:-2]):
        out[pl.ds(group ^ (2 * k), 1)] = block[...].astype(F32).T[:cap, :].astype(BF)[None]
    for k in range(0, len(refs) - 2, 2):
        pair = crossed[:, k * cap : (k + 2) * cap].astype(F32).T.astype(BF)
        out[pl.ds(group ^ (2 * k + 1), 1)] = pair[:cap, :][None]
        out[pl.ds(group ^ (2 * k + 3), 1)] = pair[cap:, :][None]


def settle(blocks, cap):
    width = blocks[0].shape[0]
    others = call(
        gather_body, "gather", list(blocks), 0, [((width, len(blocks) * cap), BF)], []
    )[0]
    return call(
        settle_body,
        "settle",
        [*blocks, hop(others, "grp", 1)],
        0,
        [((2 * len(blocks), cap, width), BF)],
        [],
    )[0]


def shards(tokens, segment, ln_gain, w_qkv, w_out, merge_gain, w_merge, owner):
    row_count, local_width = tokens.shape
    tp_count = lax.axis_size("tp")
    grp_count = lax.axis_size("grp")
    full_width = local_width * tp_count
    half = row_count // 2
    square = tp_count == 4
    partner = grp_count // 2
    n_out = 4 if square else 1
    after = lambda x, *first: lax.optimization_barrier((x, *first))[0]

    tall = tokens.T
    spans = ((0, half), (half, row_count))
    h0, h1 = split(tall, spans)
    merged_count = row_count // 4
    cap_slots = max(2, merged_count // grp_count * 2)
    crossing = grp_count == 8
    w_back, w_tall, gain, merge_wide, dispatch, ids_row = prepare(
        w_out,
        w_merge.reshape(4 * local_width, full_width),
        ln_gain,
        merge_gain,
        owner,
        segment[None, :],
        grp_count * cap_slots,
        crossing,
    )
    w_in = jnp.swapaxes(w_qkv, 1, 2).reshape(3 * local_width, full_width)

    def keys_of(pieces, start):
        return project(pieces, n_out, half, gain, w_in, far_segment[None, :], (1, 2), start)

    def own_of(pieces):
        return project(
            pieces, n_out, row_count, gain, w_in, ids_row, (0, 1, 2), 0
        )

    if square:
        mid = local_width // 2
        a = hop(tall, "tp", 1)
        b = hop(tall, "tp", 2)
        z0 = hop(h0, "grp", partner)
        c = hop(after(a, w_back)[:mid], "tp", 2)
        d = hop(b[mid:], "tp", 1)
        z1 = hop(after(h1, z0), "grp", partner)
        q, k, v = own_of(
            [
                (h0, 0, 0, 0),
                (h1, 0, 0, half),
                (a, 1, 0, 0),
                (b, 2, 0, 0),
                (c, 3, 0, 0),
                (d, 3, mid, 0),
            ]
        )
        z0 = after(z0, c, d)
        za0 = hop(z0, "tp", 1)
        zb0 = hop(z0, "tp", 2)
        z1 = after(z1, k, za0, zb0)
        za1 = hop(z1, "tp", 1)
        zb1 = hop(z1, "tp", 2)
        ta0, tb0 = za0[:mid], zb0[mid:]
        zc0 = hop(ta0, "tp", 2)
        zd0 = hop(tb0, "tp", 1)
        states = near(segment, after(q, z1, ta0, tb0), k, v)
        far_segment = hop(segment, "grp", partner)
        za1, zb1, far_segment = after((za1, zb1, far_segment), states[0][1])
        ta1, tb1 = za1[:mid], zb1[mid:]
        zc1 = hop(ta1, "tp", 2)
        zd1 = hop(tb1, "tp", 1)
        far0 = keys_of(
            [(z0, 0, 0, 0), (za0, 1, 0, 0), (zb0, 2, 0, 0), (zc0, 3, 0, 0), (zd0, 3, mid, 0)],
            0,
        )
        far1 = keys_of(
            [(z1, 0, 0, 0), (za1, 1, 0, 0), (zb1, 2, 0, 0), (zc1, 3, 0, 0), (zd1, 3, mid, 0)],
            half,
        )
    else:
        far_segment = hop(segment, "grp", partner)
        q, k, v = own_of([(lax.all_gather(tall, "tp", axis=0, tiled=True), 0, 0, 0)])
        far_whole = lax.all_gather(hop(tall, "grp", partner), "tp", axis=0, tiled=True)
        far0, far1 = [keys_of([(far_whole[:, lo:hi], 0, 0, 0)], lo) for lo, hi in spans]
        states = near(segment, q, k, v)

    states = middle(segment, far_segment, q, *far0, states, 0)
    ctx, *corners = last(segment, far_segment, q, *far1, states, w_back, n_out, half)

    halves = [h0, h1]
    if square:
        hops = ((1, 2), (2, 1))
        corners = [hop(t, "tp", side_hop) for t, (side_hop, _) in zip(corners, hops)]
        groups = []
        for i, terms in enumerate(rest(ctx, w_back, n_out, 2)):
            side_hop, next_hop = hops[i]
            side = hop(terms[side_hop], "tp", side_hop)
            passed = (terms[next_hop].astype(F32) + corners[i].astype(F32)).astype(BF)
            onward = hop(passed, "tp", next_hop)
            groups.append((halves[i], terms[0], side, onward))
    else:
        groups = [
            (h, lax.psum_scatter(t, "tp", scatter_dimension=0, tiled=True))
            for h, t in zip(halves, corners)
        ]
    hidden_out, hidden, stats = hidden_sum(groups)
    if square:
        all_stats = [stats] + [hop(stats, "tp", n) for n in (1, 2, 3)]
    else:
        gathered = lax.all_gather(stats, "tp")
        all_stats = [gathered[n] for n in range(tp_count)]
    merge_terms = merge(hidden, all_stats, merge_wide, w_tall, n_out)
    if square:
        received = [hop(merge_terms[n], "tp", n) for n in (3, 1, 2)] + [merge_terms[0]]
    else:
        received = [lax.psum_scatter(merge_terms[0], "tp", scatter_dimension=0, tiled=True)]
    if crossing:
        blocks = place(received, dispatch, grp_count // 2)
        blocks = [blocks[0]] + [
            hop(block, "grp", 2 * n) for n, block in enumerate(blocks) if n > 0
        ]
        routed = settle(blocks, cap_slots)
    else:
        outgoing = place(received, dispatch, 1)[0].reshape(grp_count, cap_slots, local_width)
        routed = lax.all_to_all(outgoing, "grp", split_axis=0, concat_axis=0, tiled=True)
    return (hidden_out.T, routed[None])


def solution(mesh):
    return jax.shard_map(
        shards,
        mesh=mesh,
        in_specs=(
            P("grp", "tp"),
            P("grp"),
            P(),
            P(None, None, "tp"),
            P("tp", None),
            P(),
            P(None, "tp", None),
            P("grp", None),
        ),
        out_specs=(P("grp", "tp"), P("grp", None, None, "tp")),
        check_vma=False,
    )
```

```python
import functools
import math

import jax
import jax.numpy as jnp
from jax import lax
from jax.experimental import pallas as pl
from jax.experimental.pallas import tpu as pltpu
from jax.sharding import PartitionSpec as P

HD = 80
HEAD_ROWS = 96
PAD = 128
FAR = 2.0**100
EPS = 1e-06
BLOCK = 256
BF = jnp.bfloat16
F32 = jnp.float32
VM = pl.BlockSpec(memory_space=pltpu.VMEM)
SM = pl.BlockSpec(memory_space=pltpu.SMEM)
HB = pl.BlockSpec(memory_space=pltpu.HBM)


def hop(x, axis, distance):
    return lax.ppermute(x, axis, [(i, i ^ distance) for i in range(lax.axis_size(axis))])


def nearby(count):
    if count == 1:
        return [0]
    me = lax.axis_index("tp")
    return [me ^ k for k in range(count)]


def call(body, name, args, smem, outs, scratch, loose=()):
    def place(i):
        if i < smem:
            return SM
        return HB if i in loose else VM

    return pl.pallas_call(
        body,
        in_specs=[place(i) for i in range(len(args))],
        out_specs=[VM for _ in outs],
        out_shape=[jax.ShapeDtypeStruct(s, d) for s, d in outs],
        scratch_shapes=scratch,
        compiler_params=pltpu.CompilerParams(vmem_limit_bytes=16 << 20),
        cost_estimate=pl.CostEstimate(flops=0, bytes_accessed=0, transcendentals=0),
        name=name,
    )(*args)


def prepare_body(
    crossing, w, w_merge, gain, merge_gain, owner, ids, *outs
):
    w_back, w_tall, gain_wide, merge_wide, dispatch, ids_row, pick = outs
    row = lax.broadcasted_iota(jnp.int32, pick.shape, 0)
    col = lax.broadcasted_iota(jnp.int32, pick.shape, 1)
    fourth = pick.shape[0] // 4
    pick[...] = jnp.where(4 * (row % fourth) + row // fourth == col, 1.0, 0.0).astype(BF)
    ids_row[...] = ids[...]
    full = w.shape[1]
    for lo in range(0, full, PAD):
        at = slice(lo, lo + PAD)
        w_back[at, :] = w[:, at].astype(F32).T.astype(BF)
        gain_wide[at, :] = jnp.broadcast_to(gain[:, at], (PAD, PAD)).T
        merge_wide[at, :] = jnp.broadcast_to(merge_gain[:, at], (PAD, PAD)).T
        for low in range(0, w_merge.shape[0], 4 * PAD):
            high = min(low + 4 * PAD, w_merge.shape[0])
            w_tall[at, low:high] = w_merge[low:high, at].astype(F32).T.astype(BF)
    slots, count = dispatch.shape
    groups = lax.axis_size("grp")
    named = owner[...]
    if crossing:
        named = named ^ lax.axis_index("grp")
    onehot = jnp.broadcast_to(named, (groups, count)) == lax.broadcasted_iota(
        jnp.int32, (groups, count), 0
    )
    before = lax.broadcasted_iota(jnp.int32, (count, count), 0) < lax.broadcasted_iota(
        jnp.int32, (count, count), 1
    )
    earlier = jnp.dot(
        jnp.where(onehot, 1.0, 0.0).astype(BF),
        jnp.where(before, 1.0, 0.0).astype(BF),
        preferred_element_type=F32,
    )
    slot = jnp.sum(jnp.where(onehot, earlier, 0.0), axis=0, keepdims=True).astype(jnp.int32)
    goal = named * (slots // groups) + slot
    dispatch[...] = jnp.where(
        lax.broadcasted_iota(jnp.int32, (slots, count), 0)
        == jnp.broadcast_to(goal, (slots, count)),
        1.0,
        0.0,
    ).astype(BF)


def prepare(w, w_merge, gain, merge_gain, owner, ids, slots, crossing):
    width, full = w.shape
    count = owner.shape[0]
    return call(
        functools.partial(prepare_body, crossing),
        "prepare",
        [w, w_merge, gain[None, :], merge_gain[None, :], owner.reshape(1, count), ids],
        0,
        [
            ((full, width), BF),
            (w_merge.shape[::-1], BF),
            ((full, PAD), F32),
            ((full, PAD), F32),
            ((slots, count), BF),
            (ids.shape, jnp.int32),
            ((ids.shape[1] // 2, ids.shape[1] // 2), BF),
        ],
        [],
    )


def split_body(spans, source, *refs):
    outs, sem = refs[:-1], refs[-1]
    copies = [
        pltpu.make_async_copy(source.at[:, lo:hi], out, sem.at[i])
        for i, ((lo, hi), out) in enumerate(zip(spans, outs))
    ]
    for copy in copies:
        copy.start()
    for copy in copies:
        copy.wait()


def split(x, spans):
    return call(
        functools.partial(split_body, spans),
        "split",
        [x],
        0,
        [((x.shape[0], hi - lo), x.dtype) for lo, hi in spans],
        [pltpu.SemaphoreType.DMA((len(spans),))],
        loose=(0,),
    )


def project_body(places, n_parts, kinds, scale, id_start, *refs):
    count = len(places)
    sources = refs[:count]
    gain, w, ids = refs[count : 3 + count]
    outs = refs[3 + count : 3 + count + len(kinds)]
    order = nearby(n_parts)
    normed = refs[-1]
    full, rows = normed.shape
    width = full // n_parts
    heads = w.shape[0] // (3 * HD)

    def load(part, col):
        found = []
        for source, (own, _, r_lo) in zip(sources, places):
            if own == part and r_lo <= col < r_lo + source.shape[1]:
                found.append(source[:, col - r_lo : col - r_lo + PAD].astype(F32))
        return found[0] if len(found) == 1 else jnp.concatenate(found, axis=0)

    each = heads * HD
    line = lax.broadcasted_iota(jnp.int32, (HEAD_ROWS - HD, BLOCK), 0)
    for start in range(0, rows, BLOCK):
        for lo in range(start, start + BLOCK, PAD):
            here = slice(lo, lo + PAD)
            base = load(0, lo)[0:1, :]
            moved = 0.0
            square = 0.0
            for k in range(n_parts):
                off = load(k, lo) - base
                moved = moved + jnp.sum(off, axis=0, keepdims=True)
                square = square + jnp.sum(off * off, axis=0, keepdims=True)
            moved = moved * (1.0 / full)
            spread = jnp.maximum(square * (1.0 / full) - moved * moved, 0.0)
            center = base + moved
            inv = lax.rsqrt(spread + EPS)
            for k in range(n_parts):
                at = pl.ds(pl.multiple_of(order[k] * width, 16), width)
                normed[at, here] = ((load(k, lo) - center) * inv * gain[at, :]).astype(BF)
        there = slice(start, start + BLOCK)
        near_ids = ids[0:1, id_start + start : id_start + start + BLOCK]
        bits = (jnp.broadcast_to(near_ids, line.shape) >> (line >> 1)) & 1
        hit = bits == (line & 1)
        product = jnp.dot(
            w[kinds[0] * each : (kinds[-1] + 1) * each, :],
            normed[:, there],
            preferred_element_type=F32,
        )
        for i, (kind, out) in enumerate(zip(kinds, outs)):
            acc = product[i * each : (i + 1) * each, :]
            if kind == 0:
                acc = acc * scale
                extra = jnp.where(hit, 0.0, -FAR)
            elif kind == 1:
                extra = jnp.where(hit, 1.0, 0.0)
            else:
                extra = jnp.where(line == 0, 1.0, 0.0)
            for h in range(heads):
                piece = acc[h * HD : (h + 1) * HD, :]
                if kind == 1:
                    tall = jnp.concatenate(
                        [piece, extra, jnp.zeros((PAD - HEAD_ROWS, BLOCK), F32)], axis=0
                    )
                    out[there, h * PAD : (h + 1) * PAD] = tall.T.astype(BF)
                else:
                    lo = h * HEAD_ROWS
                    out[lo : lo + HD, there] = piece.astype(BF)
                    out[lo + HD : lo + HEAD_ROWS, there] = extra.astype(BF)


def project(pieces, n_parts, rows, gain, w, ids, kinds, id_start):
    full = gain.shape[0]
    heads = w.shape[0] // (3 * HD)
    shape = lambda kind: (
        (rows, heads * PAD) if kind == 1 else (heads * HEAD_ROWS, rows),
        BF,
    )
    arrays = [x for x, *_ in pieces]
    places = tuple(tuple(p[1:]) for p in pieces)
    return call(
        functools.partial(
            project_body, places, n_parts, kinds, HD**-0.5 * math.log2(math.e), id_start
        ),
        "project",
        [*arrays, gain, w, ids],
        0,
        [shape(kind) for kind in kinds],
        [pltpu.VMEM((full, rows), BF)],
    )


def visit(q, kr, vr, lo, size, acc, top, cols):
    heads = q.shape[0] // HEAD_ROWS
    scores = [
        jnp.dot(
            kr[lo : lo + size, h * PAD : h * PAD + HEAD_ROWS],
            q[h * HEAD_ROWS : (h + 1) * HEAD_ROWS, :],
            preferred_element_type=F32,
        )
        for h in range(heads)
    ]
    for h, s in enumerate(scores):
        at = slice(h * HEAD_ROWS, (h + 1) * HEAD_ROWS)
        old = top[h : h + 1, cols]
        new = jnp.maximum(old, jnp.max(s, axis=0, keepdims=True))
        p = jnp.exp2(s - new).astype(BF)
        acc[at, cols] = acc[at, cols] * jnp.exp2(old - new) + jnp.dot(
            vr[at, lo : lo + size], p, preferred_element_type=F32
        )
        top[h : h + 1, cols] = new


def sweep(block, q_ids, k_ids, k_start, q, q_start, kr, vr, acc, top):
    for col in range(0, acc.shape[1], block):
        row = q_start + col
        for lo in range(0, kr.shape[0], BLOCK):
            meets = (k_ids[k_start + lo] <= q_ids[row + block - 1]) & (
                k_ids[k_start + lo + BLOCK - 1] >= q_ids[row]
            )

            @pl.when(meets)
            def _(col=col, row=row, lo=lo):
                visit(
                    q[:, row : row + block], kr, vr, lo, BLOCK, acc, top,
                    slice(col, col + block),
                )


def near_body(block, q_ids, q, k, v, *refs):
    for i in range(0, len(refs), 2):
        acc, top = refs[i : i + 2]
        acc[...] = jnp.zeros_like(acc)
        top[...] = jnp.full_like(top, -1e20)
        sweep(block, q_ids, q_ids, 0, q, i // 2 * acc.shape[1], k, v, acc, top)


def near(q_ids, q, k, v):
    wide, rows = q.shape
    a0, t0, a1, t1 = call(
        functools.partial(near_body, 2 * BLOCK),
        "near",
        [q_ids, q, k, v],
        1,
        [((wide, rows // 2), F32), ((8, rows // 2), F32)] * 2,
        [],
    )
    return [(a0, t0), (a1, t1)]


def middle_body(k_start, q_ids, k_ids, q, k, v, *refs):
    count = len(refs) // 4
    for i in range(count):
        acc_in, top_in = refs[2 * i : 2 * i + 2]
        acc, top = refs[2 * (count + i) : 2 * (count + i) + 2]
        acc[...] = acc_in[...]
        top[...] = top_in[...]
        sweep(BLOCK, q_ids, k_ids, k_start, q, i * acc.shape[1], k, v, acc, top)


def middle(q_ids, k_ids, q, k, v, states, k_start):
    flat = [x for state in states for x in state]
    found = call(
        functools.partial(middle_body, k_start),
        "middle",
        [q_ids, k_ids, q, k, v, *flat],
        2,
        [(x.shape, F32) for x in flat],
        [],
    )
    return [tuple(found[2 * i : 2 * i + 2]) for i in range(len(states))]


def multiply(w, index, width, ctx):
    at = pl.ds(pl.multiple_of(index * width, 16), width)
    return jnp.dot(w[at, :], ctx, preferred_element_type=F32).astype(BF)


def last_body(count, n_out, k_start, q_ids, k_ids, q, k, v, w, *refs):
    states = refs[: 2 * count]
    ctx = refs[2 * count]
    outs = refs[2 * count + 1 : 3 * count + 1]
    acc, top = refs[3 * count + 1 :]
    rows = acc.shape[1]
    heads = q.shape[0] // HEAD_ROWS
    order = nearby(n_out)
    for i in range(count):
        at = slice(i * rows, (i + 1) * rows)
        acc[...] = states[2 * i][...]
        top[...] = states[2 * i + 1][...]
        sweep(BLOCK, q_ids, k_ids, k_start, q, i * rows, k, v, acc, top)
        for h in range(heads):
            lo = h * HEAD_ROWS
            ctx[h * HD : (h + 1) * HD, at] = (
                acc[lo : lo + HD, :] / acc[lo + HD : lo + HD + 1, :]
            ).astype(BF)
        outs[i][...] = multiply(w, order[-1], outs[i].shape[0], ctx[:, at])


def last(q_ids, k_ids, q, k, v, states, w, n_out, k_start):
    wide, rows = q.shape
    count = len(states)
    part = rows // count
    return call(
        functools.partial(last_body, count, n_out, k_start),
        "last",
        [q_ids, k_ids, q, k, v, w, *[x for state in states for x in state]],
        2,
        [((w.shape[1], rows), BF)] + [((w.shape[0] // n_out, part), BF) for _ in states],
        [pltpu.VMEM((wide, part), F32), pltpu.VMEM((8, part), F32)],
    )


def rest_body(n_out, ctx, w, *outs):
    order = nearby(n_out)
    count = len(outs) // (n_out - 1)
    rows = ctx.shape[1] // count
    for j in range(n_out - 1):
        found = multiply(w, order[j], outs[0].shape[0], ctx[...])
        for i in range(count):
            outs[j * count + i][...] = found[:, i * rows : (i + 1) * rows]


def rest(ctx, w, n_out, count):
    found = call(
        functools.partial(rest_body, n_out),
        "rest",
        [ctx, w],
        0,
        [
            ((w.shape[0] // n_out, ctx.shape[1] // count), BF)
            for _ in range((n_out - 1) * count)
        ],
        [],
    )
    return [[found[j * count + i] for j in range(n_out - 1)] for i in range(count)]


def hidden_body(n_half, *refs):
    hidden, again, stats = refs[-3:]
    inputs = refs[:-3]
    each = len(inputs) // n_half
    rows = hidden.shape[1] // n_half
    for i in range(n_half):
        for lo in range(0, rows, PAD):
            at = slice(i * rows + lo, i * rows + lo + PAD)
            total = 0.0
            for g in inputs[i * each : (i + 1) * each]:
                total = total + g[:, lo : lo + PAD].astype(F32)
            rounded = total.astype(BF)
            hidden[:, at] = rounded
            again[:, at] = rounded
            values = rounded.astype(F32)
            center = jnp.mean(values, axis=0, keepdims=True)
            spread = jnp.mean((values - center) ** 2, axis=0, keepdims=True)
            stats[:, at] = jnp.concatenate(
                [center, spread, jnp.zeros((6, PAD), F32)], axis=0
            )


def hidden_sum(groups):
    width, rows = groups[0][0].shape
    count = rows * len(groups)
    return call(
        functools.partial(hidden_body, len(groups)),
        "hidden",
        [x for g in groups for x in g],
        0,
        [((width, count), BF), ((width, count), BF), ((8, count), F32)],
        [],
    )


def fold_body(*refs):
    out = refs[-1]
    for lo in range(0, out.shape[1], PAD):
        at = slice(lo, lo + PAD)
        total = refs[0][:, at].astype(F32)
        for r in refs[1:-1]:
            total = total + r[:, at].astype(F32)
        out[:, at] = total


def fold(*terms):
    return call(fold_body, "fold", list(terms), 0, [(terms[0].shape, F32)], [])[0]


def merge_body(n_stats, n_out, source, *refs):
    stats = refs[:n_stats]
    gain, pick, w = refs[n_stats : n_stats + 3]
    outs = refs[n_stats + 3 : n_stats + 3 + n_out]
    scaled, blocks = refs[-2:]
    width, rows = source.shape
    me = lax.axis_index("tp")
    own_gain = gain[pl.ds(pl.multiple_of(me * width, 16), width), :]
    for lo in range(0, rows, PAD):
        at = slice(lo, lo + PAD)
        means = [s[0:1, at] for s in stats]
        center = sum(means) * (1.0 / n_stats)
        spread = sum(
            s[1:2, at] + (m - center) ** 2 for s, m in zip(stats, means)
        ) * (1.0 / n_stats)
        inv = lax.rsqrt(spread + EPS)
        scaled[:, at] = ((source[:, at].astype(F32) - center) * inv * own_gain).astype(BF)
    size = pick.shape[0]
    quarter = size // 4
    for lo in range(0, rows, size):
        picked = lax.dot_general(
            pick[...],
            scaled[:, lo : lo + size],
            (((1,), (1,)), ((), ())),
            preferred_element_type=F32,
        ).astype(BF)
        for j in range(4):
            blocks[lo // 4 : lo // 4 + quarter, j * width : (j + 1) * width] = picked[
                j * quarter : (j + 1) * quarter, :
            ]
    order = nearby(n_out)
    for j in range(n_out):
        tall = outs[j].shape[0]
        at = pl.ds(pl.multiple_of(order[j] * tall, 16), tall)
        outs[j][...] = lax.dot_general(
            w[at, :], blocks[...], (((1,), (1,)), ((), ())), preferred_element_type=F32
        ).astype(BF)


def merge(hidden, stats, gain, pick, w, n_out):
    width, rows = hidden.shape
    full = w.shape[0]
    return call(
        functools.partial(merge_body, len(stats), n_out),
        "merge",
        [hidden, *stats, gain, pick, w],
        0,
        [((full // n_out, rows // 4), BF) for _ in range(n_out)],
        [
            pltpu.VMEM((width, rows), BF),
            pltpu.VMEM((rows // 4, 4 * width), BF),
        ],
    )


def place_body(n_in, *refs):
    merged = sum(r[...].astype(F32) for r in refs[:n_in]).astype(BF)
    dispatch = refs[n_in]
    outs = refs[n_in + 1 :]
    dims = (((1,), (1,)), ((), ()))
    if len(outs) == 1:
        outs[0][...] = lax.dot_general(
            dispatch[...], merged, dims, preferred_element_type=F32
        ).astype(BF)
        return
    placed = lax.dot_general(merged, dispatch[...], dims, preferred_element_type=F32)
    for k, out in enumerate(outs):
        size = out.shape[1]
        out[...] = placed[:, k * size : (k + 1) * size].astype(BF)


def place(terms, dispatch, n_out):
    slots = dispatch.shape[0]
    width = terms[0].shape[0]
    return call(
        functools.partial(place_body, len(terms)),
        "place",
        [*terms, dispatch],
        0,
        [((width, slots // n_out) if n_out > 1 else (slots, width), BF) for _ in range(n_out)],
        [],
    )


def gather_body(*refs):
    out = refs[-1]
    cap = out.shape[1] // (len(refs) - 1)
    for k, block in enumerate(refs[:-1]):
        out[:, k * cap : (k + 1) * cap] = block[:, cap:]


def settle_body(*refs):
    crossed, out = refs[-2:]
    cap = out.shape[1]
    group = lax.axis_index("grp")
    for k, block in enumerate(refs[:-2]):
        out[pl.ds(group ^ (2 * k), 1)] = block[...].astype(F32).T[:cap, :].astype(BF)[None]
    for k in range(0, len(refs) - 2, 2):
        pair = crossed[:, k * cap : (k + 2) * cap].astype(F32).T.astype(BF)
        out[pl.ds(group ^ (2 * k + 1), 1)] = pair[:cap, :][None]
        out[pl.ds(group ^ (2 * k + 3), 1)] = pair[cap:, :][None]


def settle(blocks, cap):
    width = blocks[0].shape[0]
    others = call(
        gather_body, "gather", list(blocks), 0, [((width, len(blocks) * cap), BF)], []
    )[0]
    return call(
        settle_body,
        "settle",
        [*blocks, hop(others, "grp", 1)],
        0,
        [((2 * len(blocks), cap, width), BF)],
        [],
    )[0]


def shards(tokens, segment, ln_gain, w_qkv, w_out, merge_gain, w_merge, owner):
    row_count, local_width = tokens.shape
    tp_count = lax.axis_size("tp")
    grp_count = lax.axis_size("grp")
    full_width = local_width * tp_count
    half = row_count // 2
    square = tp_count == 4
    partner = grp_count // 2
    n_out = 4 if square else 1
    after = lambda x, *first: lax.optimization_barrier((x, *first))[0]

    tall = tokens.T
    spans = ((0, half), (half, row_count))
    h0, h1 = split(tall, spans)
    merged_count = row_count // 4
    cap_slots = max(2, merged_count // grp_count * 2)
    crossing = grp_count == 8
    w_back, w_tall, gain, merge_wide, dispatch, ids_row, pick = prepare(
        w_out,
        w_merge.reshape(4 * local_width, full_width),
        ln_gain,
        merge_gain,
        owner,
        segment[None, :],
        grp_count * cap_slots,
        crossing,
    )
    w_in = jnp.swapaxes(w_qkv, 1, 2).reshape(3 * local_width, full_width)

    def keys_of(pieces, start):
        return project(pieces, n_out, half, gain, w_in, far_segment[None, :], (1, 2), start)

    def own_of(pieces):
        return project(
            pieces, n_out, row_count, gain, w_in, ids_row, (0, 1, 2), 0
        )

    if square:
        mid = local_width // 2
        a = hop(tall, "tp", 1)
        b = hop(tall, "tp", 2)
        z0 = hop(h0, "grp", partner)
        far_segment = hop(segment, "grp", partner)
        c = hop(after(a, w_back)[:mid], "tp", 2)
        d = hop(b[mid:], "tp", 1)
        z1 = hop(h1, "grp", partner)
        q, k, v = own_of(
            [
                (h0, 0, 0, 0),
                (h1, 0, 0, half),
                (a, 1, 0, 0),
                (b, 2, 0, 0),
                (c, 3, 0, 0),
                (d, 3, mid, 0),
            ]
        )
        z0 = after(z0, c, d)
        za0 = hop(z0, "tp", 1)
        zb0 = hop(z0, "tp", 2)
        z1 = after(z1, k, za0, zb0)
        za1 = hop(z1, "tp", 1)
        zb1 = hop(z1, "tp", 2)
        ta0, tb0 = za0[:mid], zb0[mid:]
        zc0 = hop(ta0, "tp", 2)
        zd0 = hop(tb0, "tp", 1)
        states = near(segment, after(q, z1, ta0, tb0), k, v)
        za1, zb1, far_segment = after((za1, zb1, far_segment), states[0][1])
        ta1, tb1 = za1[:mid], zb1[mid:]
        zc1 = hop(ta1, "tp", 2)
        zd1 = hop(tb1, "tp", 1)
        far0 = keys_of(
            [(z0, 0, 0, 0), (za0, 1, 0, 0), (zb0, 2, 0, 0), (zc0, 3, 0, 0), (zd0, 3, mid, 0)],
            0,
        )
        far1 = keys_of(
            [(z1, 0, 0, 0), (za1, 1, 0, 0), (zb1, 2, 0, 0), (zc1, 3, 0, 0), (zd1, 3, mid, 0)],
            half,
        )
    else:
        far_segment = hop(segment, "grp", partner)
        q, k, v = own_of([(lax.all_gather(tall, "tp", axis=0, tiled=True), 0, 0, 0)])
        far_whole = lax.all_gather(hop(tall, "grp", partner), "tp", axis=0, tiled=True)
        far0, far1 = [keys_of([(far_whole[:, lo:hi], 0, 0, 0)], lo) for lo, hi in spans]
        states = near(segment, q, k, v)

    states = middle(segment, far_segment, q, *far0, states, 0)
    ctx, *corners = last(segment, far_segment, q, *far1, states, w_back, n_out, half)

    halves = [h0, h1]
    if square:
        hops = ((1, 2), (2, 1))
        corners = [hop(t, "tp", side_hop) for t, (side_hop, _) in zip(corners, hops)]
        groups = []
        for i, terms in enumerate(rest(ctx, w_back, n_out, 2)):
            side_hop, next_hop = hops[i]
            side = hop(terms[side_hop], "tp", side_hop)
            passed = (terms[next_hop].astype(F32) + corners[i].astype(F32)).astype(BF)
            onward = hop(passed, "tp", next_hop)
            groups.append((fold(halves[i], terms[0], side), onward))
        sums = [g[0] for g in groups]
        groups = [(partial, after(onward, *sums)) for partial, onward in groups]
    else:
        groups = [
            (h, lax.psum_scatter(t, "tp", scatter_dimension=0, tiled=True))
            for h, t in zip(halves, corners)
        ]
    hidden_out, hidden, stats = hidden_sum(groups)
    if square:
        all_stats = [stats] + [hop(stats, "tp", n) for n in (1, 2, 3)]
    else:
        gathered = lax.all_gather(stats, "tp")
        all_stats = [gathered[n] for n in range(tp_count)]
    merge_terms = merge(hidden, all_stats, merge_wide, pick, w_tall, n_out)
    if square:
        received = [hop(merge_terms[n], "tp", n) for n in (3, 1, 2)] + [merge_terms[0]]
    else:
        received = [lax.psum_scatter(merge_terms[0], "tp", scatter_dimension=0, tiled=True)]
    if crossing:
        blocks = place(received, dispatch, grp_count // 2)
        blocks = [blocks[0]] + [
            hop(block, "grp", 2 * n) for n, block in enumerate(blocks) if n > 0
        ]
        routed = settle(blocks, cap_slots)
    else:
        outgoing = place(received, dispatch, 1)[0].reshape(grp_count, cap_slots, local_width)
        routed = lax.all_to_all(outgoing, "grp", split_axis=0, concat_axis=0, tiled=True)
    return (hidden_out.T, routed[None])


def solution(mesh):
    return jax.shard_map(
        shards,
        mesh=mesh,
        in_specs=(
            P("grp", "tp"),
            P("grp"),
            P(),
            P(None, None, "tp"),
            P("tp", None),
            P(),
            P(None, "tp", None),
            P("grp", None),
        ),
        out_specs=(P("grp", "tp"), P("grp", None, None, "tp")),
        check_vma=False,
    )
```

```python
import functools
import math

import jax
import jax.numpy as jnp
from jax import lax
from jax.experimental import pallas as pl
from jax.experimental.pallas import tpu as pltpu
from jax.sharding import PartitionSpec as P

HD = 80
HEAD_ROWS = 96
PAD = 128
FAR = 2.0**100
EPS = 1e-06
BLOCK = 256
BF = jnp.bfloat16
F32 = jnp.float32
VM = pl.BlockSpec(memory_space=pltpu.VMEM)
SM = pl.BlockSpec(memory_space=pltpu.SMEM)
HB = pl.BlockSpec(memory_space=pltpu.HBM)


def hop(x, axis, distance):
    return lax.ppermute(x, axis, [(i, i ^ distance) for i in range(lax.axis_size(axis))])


def nearby(count):
    if count == 1:
        return [0]
    me = lax.axis_index("tp")
    return [me ^ k for k in range(count)]


def call(body, name, args, smem, outs, scratch, loose=(), alias=None):
    def place(i):
        if i < smem:
            return SM
        return HB if i in loose else VM

    return pl.pallas_call(
        body,
        in_specs=[place(i) for i in range(len(args))],
        out_specs=[VM for _ in outs],
        out_shape=[jax.ShapeDtypeStruct(s, d) for s, d in outs],
        scratch_shapes=scratch,
        input_output_aliases=alias or {},
        compiler_params=pltpu.CompilerParams(vmem_limit_bytes=16 << 20),
        cost_estimate=pl.CostEstimate(flops=0, bytes_accessed=0, transcendentals=0),
        name=name,
    )(*args)


def prepare_body(
    crossing, w, w_merge, gain, merge_gain, owner, ids, *outs
):
    w_back, w_tall, gain_wide, merge_wide, dispatch, ids_row, pick = outs
    row = lax.broadcasted_iota(jnp.int32, pick.shape, 0)
    col = lax.broadcasted_iota(jnp.int32, pick.shape, 1)
    fourth = pick.shape[0] // 4
    pick[...] = jnp.where(4 * (row % fourth) + row // fourth == col, 1.0, 0.0).astype(BF)
    ids_row[...] = ids[...]
    full = w.shape[1]
    for lo in range(0, full, PAD):
        at = slice(lo, lo + PAD)
        w_back[at, :] = w[:, at].astype(F32).T.astype(BF)
        gain_wide[at, :] = jnp.broadcast_to(gain[:, at], (PAD, PAD)).T
        merge_wide[at, :] = jnp.broadcast_to(merge_gain[:, at], (PAD, PAD)).T
        for low in range(0, w_merge.shape[0], 4 * PAD):
            high = min(low + 4 * PAD, w_merge.shape[0])
            w_tall[at, low:high] = w_merge[low:high, at].astype(F32).T.astype(BF)
    slots, count = dispatch.shape
    groups = lax.axis_size("grp")
    named = owner[...]
    if crossing:
        named = named ^ lax.axis_index("grp")
    onehot = jnp.broadcast_to(named, (groups, count)) == lax.broadcasted_iota(
        jnp.int32, (groups, count), 0
    )
    before = lax.broadcasted_iota(jnp.int32, (count, count), 0) < lax.broadcasted_iota(
        jnp.int32, (count, count), 1
    )
    earlier = jnp.dot(
        jnp.where(onehot, 1.0, 0.0).astype(BF),
        jnp.where(before, 1.0, 0.0).astype(BF),
        preferred_element_type=F32,
    )
    slot = jnp.sum(jnp.where(onehot, earlier, 0.0), axis=0, keepdims=True).astype(jnp.int32)
    goal = named * (slots // groups) + slot
    dispatch[...] = jnp.where(
        lax.broadcasted_iota(jnp.int32, (slots, count), 0)
        == jnp.broadcast_to(goal, (slots, count)),
        1.0,
        0.0,
    ).astype(BF)


def prepare(w, w_merge, gain, merge_gain, owner, ids, slots, crossing):
    width, full = w.shape
    count = owner.shape[0]
    return call(
        functools.partial(prepare_body, crossing),
        "prepare",
        [w, w_merge, gain[None, :], merge_gain[None, :], owner.reshape(1, count), ids],
        0,
        [
            ((full, width), BF),
            (w_merge.shape[::-1], BF),
            ((full, PAD), F32),
            ((full, PAD), F32),
            ((slots, count), BF),
            (ids.shape, jnp.int32),
            ((ids.shape[1] // 2, ids.shape[1] // 2), BF),
        ],
        [],
    )


def split_body(spans, source, *refs):
    outs, sem = refs[:-1], refs[-1]
    copies = [
        pltpu.make_async_copy(source.at[:, lo:hi], out, sem.at[i])
        for i, ((lo, hi), out) in enumerate(zip(spans, outs))
    ]
    for copy in copies:
        copy.start()
    for copy in copies:
        copy.wait()


def split(x, spans):
    return call(
        functools.partial(split_body, spans),
        "split",
        [x],
        0,
        [((x.shape[0], hi - lo), x.dtype) for lo, hi in spans],
        [pltpu.SemaphoreType.DMA((len(spans),))],
        loose=(0,),
    )


def project_body(places, n_parts, kinds, scale, id_start, *refs):
    count = len(places)
    sources = refs[:count]
    gain, w, ids = refs[count : 3 + count]
    outs = refs[3 + count : 3 + count + len(kinds)]
    order = nearby(n_parts)
    normed = refs[-1]
    full, rows = normed.shape
    width = full // n_parts
    heads = w.shape[0] // (3 * HD)

    def load(part, col):
        found = []
        for source, (own, _, r_lo) in zip(sources, places):
            if own == part and r_lo <= col < r_lo + source.shape[1]:
                found.append(source[:, col - r_lo : col - r_lo + PAD].astype(F32))
        return found[0] if len(found) == 1 else jnp.concatenate(found, axis=0)

    each = heads * HD
    line = lax.broadcasted_iota(jnp.int32, (HEAD_ROWS - HD, BLOCK), 0)
    for start in range(0, rows, BLOCK):
        for lo in range(start, start + BLOCK, PAD):
            here = slice(lo, lo + PAD)
            base = load(0, lo)[0:1, :]
            moved = 0.0
            square = 0.0
            for k in range(n_parts):
                off = load(k, lo) - base
                moved = moved + jnp.sum(off, axis=0, keepdims=True)
                square = square + jnp.sum(off * off, axis=0, keepdims=True)
            moved = moved * (1.0 / full)
            spread = jnp.maximum(square * (1.0 / full) - moved * moved, 0.0)
            center = base + moved
            inv = lax.rsqrt(spread + EPS)
            for k in range(n_parts):
                at = pl.ds(pl.multiple_of(order[k] * width, 16), width)
                normed[at, here] = ((load(k, lo) - center) * inv * gain[at, :]).astype(BF)
        there = slice(start, start + BLOCK)
        near_ids = ids[0:1, id_start + start : id_start + start + BLOCK]
        bits = (jnp.broadcast_to(near_ids, line.shape) >> (line >> 1)) & 1
        hit = bits == (line & 1)
        product = jnp.dot(
            w[kinds[0] * each : (kinds[-1] + 1) * each, :],
            normed[:, there],
            preferred_element_type=F32,
        )
        for i, (kind, out) in enumerate(zip(kinds, outs)):
            acc = product[i * each : (i + 1) * each, :]
            if kind == 0:
                acc = acc * scale
                extra = jnp.where(hit, 0.0, -FAR)
            elif kind == 1:
                extra = jnp.where(hit, 1.0, 0.0)
            else:
                extra = jnp.where(line == 0, 1.0, 0.0)
            for h in range(heads):
                piece = acc[h * HD : (h + 1) * HD, :]
                if kind == 1:
                    tall = jnp.concatenate(
                        [piece, extra, jnp.zeros((PAD - HEAD_ROWS, BLOCK), F32)], axis=0
                    )
                    out[there, h * PAD : (h + 1) * PAD] = tall.T.astype(BF)
                else:
                    lo = h * HEAD_ROWS
                    out[lo : lo + HD, there] = piece.astype(BF)
                    out[lo + HD : lo + HEAD_ROWS, there] = extra.astype(BF)


def project(pieces, n_parts, rows, gain, w, ids, kinds, id_start):
    full = gain.shape[0]
    heads = w.shape[0] // (3 * HD)
    shape = lambda kind: (
        (rows, heads * PAD) if kind == 1 else (heads * HEAD_ROWS, rows),
        BF,
    )
    arrays = [x for x, *_ in pieces]
    places = tuple(tuple(p[1:]) for p in pieces)
    return call(
        functools.partial(
            project_body, places, n_parts, kinds, HD**-0.5 * math.log2(math.e), id_start
        ),
        "project",
        [*arrays, gain, w, ids],
        0,
        [shape(kind) for kind in kinds],
        [pltpu.VMEM((full, rows), BF)],
    )


def visit(q, kr, vr, lo, size, acc, top, cols):
    heads = q.shape[0] // HEAD_ROWS
    scores = [
        jnp.dot(
            kr[lo : lo + size, h * PAD : h * PAD + HEAD_ROWS],
            q[h * HEAD_ROWS : (h + 1) * HEAD_ROWS, :],
            preferred_element_type=F32,
        )
        for h in range(heads)
    ]
    for h, s in enumerate(scores):
        at = slice(h * HEAD_ROWS, (h + 1) * HEAD_ROWS)
        old = top[h : h + 1, cols]
        new = jnp.maximum(old, jnp.max(s, axis=0, keepdims=True))
        p = jnp.exp2(s - new).astype(BF)
        acc[at, cols] = acc[at, cols] * jnp.exp2(old - new) + jnp.dot(
            vr[at, lo : lo + size], p, preferred_element_type=F32
        )
        top[h : h + 1, cols] = new


def sweep(block, q_ids, k_ids, k_start, q, q_start, kr, vr, acc, top):
    for col in range(0, acc.shape[1], block):
        row = q_start + col
        for lo in range(0, kr.shape[0], BLOCK):
            meets = (k_ids[k_start + lo] <= q_ids[row + block - 1]) & (
                k_ids[k_start + lo + BLOCK - 1] >= q_ids[row]
            )

            @pl.when(meets)
            def _(col=col, row=row, lo=lo):
                visit(
                    q[:, row : row + block], kr, vr, lo, BLOCK, acc, top,
                    slice(col, col + block),
                )


def near_body(block, q_ids, q, k, v, *refs):
    for i in range(0, len(refs), 2):
        acc, top = refs[i : i + 2]
        acc[...] = jnp.zeros_like(acc)
        top[...] = jnp.full_like(top, -1e20)
        sweep(block, q_ids, q_ids, 0, q, i // 2 * acc.shape[1], k, v, acc, top)


def near(q_ids, q, k, v):
    wide, rows = q.shape
    a0, t0, a1, t1 = call(
        functools.partial(near_body, 2 * BLOCK),
        "near",
        [q_ids, q, k, v],
        1,
        [((wide, rows // 2), F32), ((8, rows // 2), F32)] * 2,
        [],
    )
    return [(a0, t0), (a1, t1)]


def middle_body(k_start, q_ids, k_ids, q, k, v, *refs):
    count = len(refs) // 4
    for i in range(count):
        acc, top = refs[2 * (count + i) : 2 * (count + i) + 2]
        sweep(BLOCK, q_ids, k_ids, k_start, q, i * acc.shape[1], k, v, acc, top)


def middle(q_ids, k_ids, q, k, v, states, k_start):
    flat = [x for state in states for x in state]
    found = call(
        functools.partial(middle_body, k_start),
        "middle",
        [q_ids, k_ids, q, k, v, *flat],
        2,
        [(x.shape, F32) for x in flat],
        [],
        alias={5 + i: i for i in range(len(flat))},
    )
    return [tuple(found[2 * i : 2 * i + 2]) for i in range(len(states))]


def multiply(w, index, width, ctx):
    at = pl.ds(pl.multiple_of(index * width, 16), width)
    return jnp.dot(w[at, :], ctx, preferred_element_type=F32).astype(BF)


def last_body(count, n_out, k_start, q_ids, k_ids, q, k, v, w, *refs):
    states = refs[: 2 * count]
    ctx = refs[2 * count]
    outs = refs[2 * count + 1 : 3 * count + 1]
    acc, top = refs[3 * count + 1 :]
    rows = acc.shape[1]
    heads = q.shape[0] // HEAD_ROWS
    order = nearby(n_out)
    for i in range(count):
        at = slice(i * rows, (i + 1) * rows)
        acc[...] = states[2 * i][...]
        top[...] = states[2 * i + 1][...]
        sweep(BLOCK, q_ids, k_ids, k_start, q, i * rows, k, v, acc, top)
        for h in range(heads):
            lo = h * HEAD_ROWS
            share = 1.0 / acc[lo + HD : lo + HD + 1, :]
            ctx[h * HD : (h + 1) * HD, at] = (acc[lo : lo + HD, :] * share).astype(BF)
        outs[i][...] = multiply(w, order[-1], outs[i].shape[0], ctx[:, at])


def last(q_ids, k_ids, q, k, v, states, w, n_out, k_start):
    wide, rows = q.shape
    count = len(states)
    part = rows // count
    return call(
        functools.partial(last_body, count, n_out, k_start),
        "last",
        [q_ids, k_ids, q, k, v, w, *[x for state in states for x in state]],
        2,
        [((w.shape[1], rows), BF)] + [((w.shape[0] // n_out, part), BF) for _ in states],
        [pltpu.VMEM((wide, part), F32), pltpu.VMEM((8, part), F32)],
    )


def rest_body(n_out, ctx, w, *outs):
    order = nearby(n_out)
    count = len(outs) // (n_out - 1)
    rows = ctx.shape[1] // count
    for j in range(n_out - 1):
        found = multiply(w, order[j], outs[0].shape[0], ctx[...])
        for i in range(count):
            outs[j * count + i][...] = found[:, i * rows : (i + 1) * rows]


def rest(ctx, w, n_out, count):
    found = call(
        functools.partial(rest_body, n_out),
        "rest",
        [ctx, w],
        0,
        [
            ((w.shape[0] // n_out, ctx.shape[1] // count), BF)
            for _ in range((n_out - 1) * count)
        ],
        [],
    )
    return [[found[j * count + i] for j in range(n_out - 1)] for i in range(count)]


def hidden_body(n_half, *refs):
    hidden, again, stats = refs[-3:]
    inputs = refs[:-3]
    each = len(inputs) // n_half
    rows = hidden.shape[1] // n_half
    for i in range(n_half):
        for lo in range(0, rows, PAD):
            at = slice(i * rows + lo, i * rows + lo + PAD)
            total = 0.0
            for g in inputs[i * each : (i + 1) * each]:
                total = total + g[:, lo : lo + PAD].astype(F32)
            rounded = total.astype(BF)
            hidden[:, at] = rounded
            again[:, at] = rounded
            values = rounded.astype(F32)
            center = jnp.mean(values, axis=0, keepdims=True)
            spread = jnp.mean((values - center) ** 2, axis=0, keepdims=True)
            stats[:, at] = jnp.concatenate(
                [center, spread, jnp.zeros((6, PAD), F32)], axis=0
            )


def hidden_sum(groups):
    width, rows = groups[0][0].shape
    count = rows * len(groups)
    return call(
        functools.partial(hidden_body, len(groups)),
        "hidden",
        [x for g in groups for x in g],
        0,
        [((width, count), BF), ((width, count), BF), ((8, count), F32)],
        [],
    )


def fold_body(*refs):
    out = refs[-1]
    for lo in range(0, out.shape[1], PAD):
        at = slice(lo, lo + PAD)
        total = refs[0][:, at].astype(F32)
        for r in refs[1:-1]:
            total = total + r[:, at].astype(F32)
        out[:, at] = total


def fold(*terms):
    return call(fold_body, "fold", list(terms), 0, [(terms[0].shape, F32)], [])[0]


def merge_body(n_stats, n_out, source, *refs):
    stats = refs[:n_stats]
    gain, pick, w = refs[n_stats : n_stats + 3]
    outs = refs[n_stats + 3 : n_stats + 3 + n_out]
    scaled, blocks = refs[-2:]
    width, rows = source.shape
    me = lax.axis_index("tp")
    own_gain = gain[pl.ds(pl.multiple_of(me * width, 16), width), :]
    for lo in range(0, rows, PAD):
        at = slice(lo, lo + PAD)
        means = [s[0:1, at] for s in stats]
        center = sum(means) * (1.0 / n_stats)
        spread = sum(
            s[1:2, at] + (m - center) ** 2 for s, m in zip(stats, means)
        ) * (1.0 / n_stats)
        inv = lax.rsqrt(spread + EPS)
        scaled[:, at] = ((source[:, at].astype(F32) - center) * inv * own_gain).astype(BF)
    size = pick.shape[0]
    quarter = size // 4
    for lo in range(0, rows, size):
        picked = lax.dot_general(
            pick[...],
            scaled[:, lo : lo + size],
            (((1,), (1,)), ((), ())),
            preferred_element_type=F32,
        ).astype(BF)
        for j in range(4):
            blocks[lo // 4 : lo // 4 + quarter, j * width : (j + 1) * width] = picked[
                j * quarter : (j + 1) * quarter, :
            ]
    order = nearby(n_out)
    for j in range(n_out):
        tall = outs[j].shape[0]
        at = pl.ds(pl.multiple_of(order[j] * tall, 16), tall)
        outs[j][...] = lax.dot_general(
            w[at, :], blocks[...], (((1,), (1,)), ((), ())), preferred_element_type=F32
        ).astype(BF)


def merge(hidden, stats, gain, pick, w, n_out):
    width, rows = hidden.shape
    full = w.shape[0]
    return call(
        functools.partial(merge_body, len(stats), n_out),
        "merge",
        [hidden, *stats, gain, pick, w],
        0,
        [((full // n_out, rows // 4), BF) for _ in range(n_out)],
        [
            pltpu.VMEM((width, rows), BF),
            pltpu.VMEM((rows // 4, 4 * width), BF),
        ],
    )


def place_body(n_in, *refs):
    merged = sum(r[...].astype(F32) for r in refs[:n_in]).astype(BF)
    dispatch = refs[n_in]
    outs = refs[n_in + 1 :]
    dims = (((1,), (1,)), ((), ()))
    if len(outs) == 1:
        outs[0][...] = lax.dot_general(
            dispatch[...], merged, dims, preferred_element_type=F32
        ).astype(BF)
        return
    placed = lax.dot_general(merged, dispatch[...], dims, preferred_element_type=F32)
    for k, out in enumerate(outs):
        size = out.shape[1]
        out[...] = placed[:, k * size : (k + 1) * size].astype(BF)


def place(terms, dispatch, n_out):
    slots = dispatch.shape[0]
    width = terms[0].shape[0]
    return call(
        functools.partial(place_body, len(terms)),
        "place",
        [*terms, dispatch],
        0,
        [((width, slots // n_out) if n_out > 1 else (slots, width), BF) for _ in range(n_out)],
        [],
    )


def gather_body(*refs):
    out = refs[-1]
    cap = out.shape[1] // (len(refs) - 1)
    for k, block in enumerate(refs[:-1]):
        out[:, k * cap : (k + 1) * cap] = block[:, cap:]


def settle_body(*refs):
    crossed, out = refs[-2:]
    cap = out.shape[1]
    group = lax.axis_index("grp")
    for k, block in enumerate(refs[:-2]):
        out[pl.ds(group ^ (2 * k), 1)] = block[...].astype(F32).T[:cap, :].astype(BF)[None]
    for k in range(0, len(refs) - 2, 2):
        pair = crossed[:, k * cap : (k + 2) * cap].astype(F32).T.astype(BF)
        out[pl.ds(group ^ (2 * k + 1), 1)] = pair[:cap, :][None]
        out[pl.ds(group ^ (2 * k + 3), 1)] = pair[cap:, :][None]


def settle(blocks, cap):
    width = blocks[0].shape[0]
    others = call(
        gather_body, "gather", list(blocks), 0, [((width, len(blocks) * cap), BF)], []
    )[0]
    return call(
        settle_body,
        "settle",
        [*blocks, hop(others, "grp", 1)],
        0,
        [((2 * len(blocks), cap, width), BF)],
        [],
    )[0]


def shards(tokens, segment, ln_gain, w_qkv, w_out, merge_gain, w_merge, owner):
    row_count, local_width = tokens.shape
    tp_count = lax.axis_size("tp")
    grp_count = lax.axis_size("grp")
    full_width = local_width * tp_count
    half = row_count // 2
    square = tp_count == 4
    partner = grp_count // 2
    n_out = 4 if square else 1
    after = lambda x, *first: lax.optimization_barrier((x, *first))[0]

    tall = tokens.T
    spans = ((0, half), (half, row_count))
    h0, h1 = split(tall, spans)
    merged_count = row_count // 4
    cap_slots = max(2, merged_count // grp_count * 2)
    crossing = grp_count == 8
    w_back, w_tall, gain, merge_wide, dispatch, ids_row, pick = prepare(
        w_out,
        w_merge.reshape(4 * local_width, full_width),
        ln_gain,
        merge_gain,
        owner,
        segment[None, :],
        grp_count * cap_slots,
        crossing,
    )
    w_in = jnp.swapaxes(w_qkv, 1, 2).reshape(3 * local_width, full_width)

    def keys_of(pieces, start):
        return project(pieces, n_out, half, gain, w_in, far_segment[None, :], (1, 2), start)

    def own_of(pieces):
        return project(
            pieces, n_out, row_count, gain, w_in, ids_row, (0, 1, 2), 0
        )

    if square:
        mid = local_width // 2
        a = hop(tall, "tp", 1)
        b = hop(tall, "tp", 2)
        z0 = hop(h0, "grp", partner)
        far_segment = hop(segment, "grp", partner)
        c = hop(after(a, w_back)[:mid], "tp", 2)
        d = hop(b[mid:], "tp", 1)
        z1 = hop(h1, "grp", partner)
        q, k, v = own_of(
            [
                (h0, 0, 0, 0),
                (h1, 0, 0, half),
                (a, 1, 0, 0),
                (b, 2, 0, 0),
                (c, 3, 0, 0),
                (d, 3, mid, 0),
            ]
        )
        z0 = after(z0, c, d)
        za0 = hop(z0, "tp", 1)
        zb0 = hop(z0, "tp", 2)
        z1 = after(z1, k, za0, zb0)
        za1 = hop(z1, "tp", 1)
        zb1 = hop(z1, "tp", 2)
        ta0, tb0 = za0[:mid], zb0[mid:]
        zc0 = hop(ta0, "tp", 2)
        zd0 = hop(tb0, "tp", 1)
        states = near(segment, after(q, z1, ta0, tb0), k, v)
        za1, zb1, far_segment = after((za1, zb1, far_segment), states[0][1])
        ta1, tb1 = za1[:mid], zb1[mid:]
        zc1 = hop(ta1, "tp", 2)
        zd1 = hop(tb1, "tp", 1)
        far0 = keys_of(
            [(z0, 0, 0, 0), (za0, 1, 0, 0), (zb0, 2, 0, 0), (zc0, 3, 0, 0), (zd0, 3, mid, 0)],
            0,
        )
        far1 = keys_of(
            [(z1, 0, 0, 0), (za1, 1, 0, 0), (zb1, 2, 0, 0), (zc1, 3, 0, 0), (zd1, 3, mid, 0)],
            half,
        )
    else:
        far_segment = hop(segment, "grp", partner)
        q, k, v = own_of([(lax.all_gather(tall, "tp", axis=0, tiled=True), 0, 0, 0)])
        far_whole = lax.all_gather(hop(tall, "grp", partner), "tp", axis=0, tiled=True)
        far0, far1 = [keys_of([(far_whole[:, lo:hi], 0, 0, 0)], lo) for lo, hi in spans]
        states = near(segment, q, k, v)

    states = middle(segment, far_segment, q, *far0, states, 0)
    ctx, *corners = last(segment, far_segment, q, *far1, states, w_back, n_out, half)

    halves = [h0, h1]
    if square:
        hops = ((1, 2), (2, 1))
        corners = [hop(t, "tp", side_hop) for t, (side_hop, _) in zip(corners, hops)]
        groups = []
        for i, terms in enumerate(rest(ctx, w_back, n_out, 2)):
            side_hop, next_hop = hops[i]
            side = hop(terms[side_hop], "tp", side_hop)
            passed = (terms[next_hop].astype(F32) + corners[i].astype(F32)).astype(BF)
            onward = hop(passed, "tp", next_hop)
            groups.append((fold(halves[i], terms[0], side), onward))
        sums = [g[0] for g in groups]
        groups = [(partial, after(onward, *sums)) for partial, onward in groups]
    else:
        groups = [
            (h, lax.psum_scatter(t, "tp", scatter_dimension=0, tiled=True))
            for h, t in zip(halves, corners)
        ]
    hidden_out, hidden, stats = hidden_sum(groups)
    if square:
        all_stats = [stats] + [hop(stats, "tp", n) for n in (1, 2, 3)]
    else:
        gathered = lax.all_gather(stats, "tp")
        all_stats = [gathered[n] for n in range(tp_count)]
    merge_terms = merge(hidden, all_stats, merge_wide, pick, w_tall, n_out)
    if square:
        received = [hop(merge_terms[n], "tp", n) for n in (3, 1, 2)] + [merge_terms[0]]
    else:
        received = [lax.psum_scatter(merge_terms[0], "tp", scatter_dimension=0, tiled=True)]
    if crossing:
        blocks = place(received, dispatch, grp_count // 2)
        blocks = [blocks[0]] + [
            hop(block, "grp", 2 * n) for n, block in enumerate(blocks) if n > 0
        ]
        routed = settle(blocks, cap_slots)
    else:
        outgoing = place(received, dispatch, 1)[0].reshape(grp_count, cap_slots, local_width)
        routed = lax.all_to_all(outgoing, "grp", split_axis=0, concat_axis=0, tiled=True)
    return (hidden_out.T, routed[None])


def solution(mesh):
    return jax.shard_map(
        shards,
        mesh=mesh,
        in_specs=(
            P("grp", "tp"),
            P("grp"),
            P(),
            P(None, None, "tp"),
            P("tp", None),
            P(),
            P(None, "tp", None),
            P("grp", None),
        ),
        out_specs=(P("grp", "tp"), P("grp", None, None, "tp")),
        check_vma=False,
    )
```
